32 devices in a mesh: det: 4 (over z), tm: 8 (over y, x, core).
Axes of the slice: x: 2, y: 2, z: 4, core: 2. Of those that a mesh axis runs over, the one named last changes fastest.
Arguments:
- timestream: bfloat16 [32, 1048576], P('det', 'tm'), may hold values from -6 to 6
- angles: float32 [32], P('det'), may hold values from -3.140625 to 3.140625
- det_weight: float32 [32], P('det'), may hold values from 0.3 to 3
- pointing: bfloat16 [1024, 64, 1024], P('tm'), may hold values from 0 to 0.03125
- owner: int32 [4, 1024, 1], P('det', 'tm'), may hold values from 0 to 31; in each aligned block of 128 rows (0 to 127, 128 to 255, ..., all dimensions but the last counted through in order) at most 8 rows name the same one
- sub_block: int32 [4, 1024], P('det', 'tm'), may hold values from 0 to 31
- cov: bfloat16 [256, 3, 256, 256], P(('det', 'tm')), may hold values from -0.21875 to 0.21875
- band: int32 [256, 3], P(('det', 'tm')), may hold values from -2 to 2
Outputs:
- map_sum: float32 [3, 65536], P(None, ('det', 'tm'))
- weighted: float32 [3, 65536], P(None, ('det', 'tm'))
The draws below stay inside these ranges and needn't reach their ends.
Inputs may be any that keep to these rules, and one draw needn't show every extreme that they name: Among the 128 tiles of one device and group no owner is named more than 8 times, a bound that some block reaches; every device owns some tile.
All inputs are finite; a program needn't handle non-finite values.
Results may differ from the reference program's by a relative error of at most 0.0051.
Values may be sent and summed in bfloat16 or wider, within the bound.
A program may use at most 64 MiB of HBM per device.

```python
import math
import jax
import jax.numpy as jnp
import numpy as np
from jax import lax

DET_DEV = 8
NT_DEV = 128
TS = 1024
PB = 64
CB = 256
H = 2
K = 3
GROUPS = 4
DETS = 32
SAMPLES = 1048576
NTILES = 1024
BPD = 32
NPIX = 65536
NBLK = 1024
NCB = 256
CAP = 8
DEVICES = 32


def with_ends(entries, rng, smallest, high):
    place = [jax.random.randint(jax.random.fold_in(rng, axis), (), 0, length) for axis, length in enumerate(entries.shape)]
    longest = entries.shape.index(max(entries.shape))
    neighbour = place[:longest] + [(place[longest] + 1) % entries.shape[longest]] + place[longest + 1:]
    return entries.at[tuple(place)].set(smallest).at[tuple(neighbour)].set(high)


def level_of(own_key, extent, split, low, top_value):
    gain = 1.0
    for dim, parts in split:
        steps = jax.random.uniform(jax.random.fold_in(jax.random.fold_in(own_key, 6), dim), (parts,), jnp.float32, low / len(split), top_value / len(split))
        gain = gain * jnp.repeat(jnp.exp(steps), extent[dim] // parts).reshape((-1,) + (1,) * (len(extent) - 1 - dim))
    return gain


def deal_out(own_key, own, number, rows, amount, top, limit, skew):
    ranking = jax.random.permutation(own_key, amount)
    heavy_load, common = load_shares(amount, rows * top, limit, skew, True), load_shares(amount, rows * top, limit, skew, False)
    places = jnp.arange(amount)

    def named(tallies, turn):
        used = int((tallies > 0).sum())
        fixed = max(1, used // 4)
        shifted = fixed + (places - fixed + turn * (used - fixed)) % max(1, amount - fixed)
        return jnp.zeros((amount,), jnp.int32).at[ranking[jnp.where(places < fixed, places, shifted)]].set(jnp.asarray(tallies, jnp.int32))

    tallies = jnp.where(number % 4 == 0, named(heavy_load, number // 4), named(common, number - number // 4 - 1))
    mixed = jax.random.permutation(jax.random.fold_in(own, 3), amount)
    source_of, sink = mixed[0:amount // 2 * 2:2], mixed[1:amount // 2 * 2:2]
    slack = jnp.minimum(tallies[source_of] - 1, limit - tallies[sink]) // 2
    slack = jnp.where((source_of == ranking[0]) | (sink == ranking[0]) | (tallies[sink] == 0), 0, jnp.maximum(slack, 0))
    shifted = jax.random.randint(jax.random.fold_in(own, 4), (amount // 2,), 0, 1 << 20) % (slack + 1)
    tallies = tallies.at[source_of].add(-shifted).at[sink].add(shifted)
    members = jnp.searchsorted(jnp.cumsum(tallies), jnp.arange(rows * top), side="right").astype(jnp.int32)
    table = members.reshape(top, rows).T
    table = table[jax.random.permutation(jax.random.fold_in(own, 1), rows)]
    turn = jax.random.randint(jax.random.fold_in(own, 2), (rows, 1), 0, top)
    return jnp.take_along_axis(table, (jnp.arange(top)[None, :] + turn) % top, axis=1)


def load_shares(count, total, limit, lean, full):
    portions = [(1 << 20) // math.isqrt(rank ** lean) + 1 for rank in range(1, count + 1)]
    largest = limit if full else min(limit, max(-(-total // count), total * portions[0] // sum(portions)))
    least = 1 if total - largest >= count - 1 else 0
    counts, surplus = [largest] + [least] * (count - 1), total - largest - least * (count - 1)
    while surplus > 0:
        movable = [i for i in range(1, count) if counts[i] < largest] or [i for i in range(1, count) if counts[i] < limit]
        whole, remaining = sum([portions[i] for i in movable]), surplus
        for i in movable:
            more = min(limit - counts[i], max(1, remaining * portions[i] // whole), surplus)
            counts[i] = counts[i] + more
            surplus = surplus - more
    return np.array(counts)


def scatter_about(stream_key, shape, deviation, bound, split=(), held_as=jnp.bfloat16):
    values = jax.random.normal(stream_key, shape, jnp.float32) * deviation
    if len(split) > 0:
        values = level_of(stream_key, shape, split, -0.22, 0.18) * values
    return jnp.clip(values, min=-bound, max=bound).astype(held_as)


def setup_inputs(seed: int = 0) -> dict:
    streams_of = jax.random.split(jax.random.key(seed), 9)
    timestream = scatter_about(streams_of[0], (DETS, SAMPLES), 1.0, 6.0, ((0, 4), (1, 8)))
    angles = jnp.clip(jax.random.uniform(streams_of[1], (DETS,), jnp.float32, -3.140625, 3.140625), -3.140625, 3.140625)
    det_weight = jnp.clip(jnp.exp(math.log(3.0) - 2.3025851 * jax.random.uniform(streams_of[2], (DETS,), jnp.float32) ** level_of(streams_of[2], (DETS,), ((0, 4),), -0.2, 0.2)), 0.3, 3.0)
    pointing = jnp.clip(0.03125 * jax.random.uniform(streams_of[3], (NTILES, PB, TS), jnp.float32) ** level_of(streams_of[3], (NTILES, PB, TS), ((0, 8),), -0.2, 0.2), 0.0, 0.03125).astype(jnp.bfloat16)
    owner_keys = jax.random.split(jax.random.fold_in(streams_of[4], 1), GROUPS * NTILES // NT_DEV)
    owner_turns = jax.random.permutation(jax.random.fold_in(streams_of[4], 3), GROUPS * NTILES // NT_DEV)
    owner = jax.vmap(lambda own, number: deal_out(jax.random.fold_in(streams_of[4], 2), own, number, NT_DEV, DEVICES, 1, CAP, 2))(owner_keys, owner_turns).reshape((GROUPS, NTILES, 1))
    sub_block = with_ends(jax.random.randint(streams_of[5], (GROUPS, NTILES), 0, BPD), jax.random.fold_in(streams_of[5], 1), 0, BPD - 1).astype(jnp.int32)
    cov = scatter_about(streams_of[6], (NCB, K, CB, CB), (K * CB) ** -0.5, 0.21875, ((0, 32),))
    band = with_ends(jax.random.randint(streams_of[7], (NCB, K), 0 - H, H + 1), jax.random.fold_in(streams_of[7], 1), 0 - H, H).astype(jnp.int32)
    return {"timestream": timestream, "angles": angles, "det_weight": det_weight, "pointing": pointing, "owner": owner, "sub_block": sub_block, "cov": cov, "band": band}


def polar_weights(angles, det_weight):
    twice = 2.0 * angles.astype(jnp.float32)
    stacked = jnp.stack([jnp.ones_like(twice), jnp.cos(twice), jnp.sin(twice)], axis=1)
    return (det_weight.astype(jnp.float32)[:, None] * stacked).astype(jnp.bfloat16)


def reference(timestream, angles, det_weight, pointing, owner, sub_block, cov, band):
    polar = polar_weights(angles, det_weight).reshape(GROUPS, DET_DEV, 3)
    stream = timestream.reshape(GROUPS, DET_DEV, SAMPLES)
    pointing_wide = pointing.astype(jnp.float32)

    def group_tiles(pair):
        polar_group, stream_group = pair
        projected = jnp.dot(polar_group.T, stream_group, preferred_element_type=jnp.float32).astype(jnp.bfloat16)
        shaped = projected.astype(jnp.float32).reshape(3, NTILES, TS)
        return jnp.einsum("skt,kpt->ksp", shaped, pointing_wide, precision=lax.Precision.HIGHEST)

    tile_maps = lax.map(group_tiles, (polar, stream))
    target = (owner[:, :, 0] * BPD + sub_block).reshape(-1).astype(jnp.int32)
    summed = jax.ops.segment_sum(tile_maps.reshape(GROUPS * NTILES, 3 * PB), target, num_segments=NBLK)
    map_sum = summed.reshape(NBLK, 3, PB).transpose(1, 0, 2).reshape(3, NPIX)
    map_half = map_sum.astype(jnp.bfloat16)
    padded = jnp.pad(map_half, ((0, 0), (H * CB, H * CB)))
    blocks = padded.reshape(3, NCB + 2 * H, CB)
    source = (jnp.arange(NCB, dtype=jnp.int32)[:, None] + H + band).astype(jnp.int32)
    gathered = jnp.take(blocks, source, axis=1)

    def apply_block(pair):
        block_cov, block_map = pair
        return jnp.einsum("jcd,sjd->sc", block_cov.astype(jnp.float32), block_map.astype(jnp.float32), precision=lax.Precision.HIGHEST)

    weighted = lax.map(apply_block, (cov, gathered.transpose(1, 0, 2, 3)))
    weighted = weighted.transpose(1, 0, 2).reshape(3, NPIX)
    return map_sum, weighted
```

```python
import functools

import jax
import jax.numpy as jnp
from jax import lax
from jax.experimental import pallas as pl
from jax.experimental.pallas import tpu as pltpu
from jax.sharding import PartitionSpec as P

H = 2
MESH = pl.DeviceIdType.MESH
NT = (((1,), (1,)), ((), ()))
F32 = jnp.float32
BF16 = jnp.bfloat16
I32 = jnp.int32


def iota(shape, dim):
    return lax.broadcasted_iota(I32, shape, dim)


def mm(a, b):
    return jnp.dot(a, b, preferred_element_type=F32)


def mm_nt(a, b):
    return lax.dot_general(a, b, NT, preferred_element_type=F32)


def kernel(
    n_det, n_tm, cap, rows,
    angles_hbm, weight_hbm, owner_hbm, sub_hbm, band_hbm, ts_hbm, pt_hbm, cov_hbm,
    both,
    angles, weight, owner, sub, band,
    ts, pt, cov, proj, tiles, pick, send, recv, ext, low, high,
    small_sem, ts_sem, pt_sem, cov_sem, send_sem, recv_sem, halo_send, halo_recv,
):
    n = n_det * n_tm
    group = 16
    tile_count = pt.shape[0]
    groups = tile_count // group
    pix = pt.shape[1]
    length = pt.shape[2]
    lanes = 2 * pix
    me = lax.axis_index("det") * n_tm + lax.axis_index("tm")

    def coords(d):
        return (d // n_tm, d % n_tm)

    small = [
        pltpu.make_async_copy(a, b, small_sem.at[i])
        for i, (a, b) in enumerate((
            (owner_hbm, owner), (sub_hbm, sub), (angles_hbm, angles), (weight_hbm, weight), (band_hbm, band),
        ))
    ]
    for copy in small:
        copy.start()
    for g in range(groups):
        span = pl.ds(g * group * length, group * length)
        pltpu.make_async_copy(ts_hbm.at[:, span], ts.at[:, span], ts_sem.at[g]).start()
    def fetch(low_g, high_g):
        for g in range(low_g, high_g):
            part = pl.ds(g * group, group)
            pltpu.make_async_copy(pt_hbm.at[part], pt.at[part], pt_sem.at[g]).start()

    fetch(0, groups * 2 // 8)
    cov_copy = pltpu.make_async_copy(cov_hbm, cov, cov_sem)

    barrier = pltpu.get_barrier_semaphore()

    def greet(i, carry):
        pl.semaphore_signal(barrier, inc=1, device_id=coords((me + i) % n), device_id_type=MESH)
        return carry

    lax.fori_loop(1, n, greet, 0)
    fetch(groups * 2 // 8, groups * 4 // 8)
    for copy in small:
        copy.wait()

    dest = jnp.broadcast_to(owner[...].astype(F32), (tile_count, tile_count))
    eye = (iota((tile_count, tile_count), 0) == iota((tile_count, tile_count), 1)).astype(BF16)
    dest_column = mm_nt(eye, dest.astype(BF16))
    earlier = iota((tile_count, tile_count), 0) < iota((tile_count, tile_count), 1)
    rank = jnp.sum(jnp.where(earlier & (dest_column == dest), 1.0, 0.0), axis=0, keepdims=True)
    twice = (iota((tile_count, 2 * tile_count), 1) // 2 == iota((tile_count, 2 * tile_count), 0)).astype(BF16)
    pair = jnp.where(iota((8, tile_count), 0) == 0, jnp.broadcast_to(owner[...].astype(F32), (8, tile_count)),
                     jnp.broadcast_to(rank, (8, tile_count))).astype(BF16)
    pair = mm(pair, twice)
    target = (pair[0:1] * rows + pair[1:2] * 2.0).astype(I32) + iota((1, 2 * tile_count), 1) % 2
    chunk = 256

    def fill(c, carry):
        base = pl.multiple_of(c * chunk, chunk)
        pick[pl.ds(base, chunk), :] = (iota((chunk, 2 * tile_count), 0) + base == target).astype(F32).astype(BF16)
        return carry

    lax.fori_loop(0, n * rows // chunk, fill, 0)

    sub_b = jnp.where(iota((lanes, tile_count), 0) >= pix,
                      jnp.broadcast_to(sub[...].astype(F32), (lanes, tile_count)), 0.0).astype(BF16)
    odd = (iota((2 * tile_count, tile_count), 0) == 2 * iota((2 * tile_count, tile_count), 1) + 1).astype(BF16)
    sub_rows = mm_nt(odd, sub_b)

    row8 = iota((8, 8), 0)
    ang = jnp.broadcast_to(2.0 * angles[...], (8, 8))
    wgt = jnp.broadcast_to(weight[...], (8, 8))
    trig = jnp.where(row8 == 0, 1.0, jnp.where(row8 == 1, jnp.cos(ang), jnp.sin(ang)))
    polar = jnp.where(row8 < 3, wgt * trig, 0.0).astype(BF16)
    r = iota((64, 8), 0)
    stokes = 2 * (r % 2) + (r // 8) % 2
    spread = mm((stokes == iota((64, 8), 1)).astype(F32).astype(BF16), polar).astype(BF16)
    spread = mm(spread, (iota((8, 128), 1) % 8 == iota((8, 128), 0)).astype(F32).astype(BF16))
    r = iota((64, 128), 0)
    tile_of = 4 * (r // 16) + (r // 2) % 4
    diagonal = jnp.where(iota((64, 128), 1) // 8 == tile_of, spread, 0.0).astype(BF16)

    row = iota((8, lanes), 0)
    left = iota((8, lanes), 1) < pix

    def project(g, carry):
        start = pl.multiple_of(g * group * length, group * length)
        span = pl.ds(start, group * length)
        pltpu.make_async_copy(ts_hbm.at[:, span], ts.at[:, span], ts_sem.at[g]).wait()
        stream = jnp.concatenate(
            [ts[:, pl.ds(pl.multiple_of(start + k * length, length), length)].astype(F32) for k in range(group)], axis=0
        ).astype(BF16)
        proj[pl.ds(pl.multiple_of(g * 64, 64), 64), :] = mm(diagonal, stream).astype(BF16)
        return carry

    fetch(groups * 4 // 8, groups * 6 // 8)
    lax.fori_loop(0, groups, project, 0)
    fetch(groups * 6 // 8, groups)
    cov_copy.start()

    def step(g, carry):
        part = pl.ds(g * group, group)
        pltpu.make_async_copy(pt_hbm.at[part], pt.at[part], pt_sem.at[g]).wait()
        for q in range(4):
            block = pt[pl.ds(g * group + 4 * q, 4)].reshape(4 * pix, length)
            out = mm_nt(proj[pl.ds(pl.multiple_of(g * 64 + 16 * q, 16), 16), :], block)
            even = jnp.where(row < 4, out[0:8, 0:lanes], out[0:8, lanes:])
            odds = jnp.where(row < 4, out[8:16, 0:lanes], out[8:16, lanes:])
            first = jnp.where(left, even, pltpu.roll(odds, pix, 1))
            second = jnp.where(left, pltpu.roll(even, pix, 1), odds)
            tiles[pl.ds(pl.multiple_of(g * 32 + 8 * q, 8), 8), :] = jnp.where((row // 2) % 2 == 0, first, second)
        return carry

    lax.fori_loop(0, groups, step, 0)

    payload = (tiles[...] + sub_rows).astype(BF16)
    send[...] = mm(pick[...], payload).astype(BF16).reshape(n, rows, lanes)

    pl.semaphore_wait(barrier, n - 1)

    def push(i, carry):
        d = (me + i) % n
        pltpu.make_async_remote_copy(
            src_ref=send.at[d], dst_ref=recv.at[me], send_sem=send_sem, recv_sem=recv_sem,
            device_id=coords(d), device_id_type=MESH,
        ).start()
        return carry

    lax.fori_loop(1, n, push, 0)
    recv[me] = send[me]
    ext[...] = jnp.zeros_like(ext)
    others = pl.ds(0, n - 1)
    pltpu.make_async_copy(recv.at[others], recv.at[others], recv_sem).wait()

    got = recv[...].reshape(n * rows, lanes)
    probe = (iota((8, lanes), 1) == pix).astype(F32).astype(BF16)
    sub_of = mm_nt(probe, got)[0:1]
    is_odd = iota((1, n * rows), 1) % 2 == 1
    sub_of = jnp.where(is_odd, sub_of, pltpu.roll(sub_of, n * rows - 1, 1)).astype(I32)
    own_blocks = both.shape[2] // pix
    half = own_blocks // 2
    r = iota((2 * own_blocks, n * rows), 0)
    wanted = 2 * (r % half) + (r // half) % 2
    hit = (wanted == jnp.broadcast_to(sub_of, r.shape)) & (r // own_blocks == iota(r.shape, 1) % 2)
    total = mm(hit.astype(F32).astype(BF16), got)
    side = iota((half, lanes), 1) < pix
    a0, a1, b0, b1 = (total[half * i:half * (i + 1)] for i in range(4))
    planes = (
        jnp.where(side, a0, pltpu.roll(a1, pix, 1)),
        jnp.where(side, pltpu.roll(a0, pix, 1), a1),
        jnp.where(side, b0, pltpu.roll(b1, pix, 1)),
    )
    block_rows, taps, cb = cov.shape[0], cov.shape[1], cov.shape[2]
    per = cb // lanes
    for s in range(3):
        rounded = planes[s].astype(BF16).astype(F32)
        for i in range(half):
            ext[H + i // per, s:s + 1, (i % per) * lanes:(i % per + 1) * lanes] = rounded[i:i + 1]

    last = n - 1

    def to_next():
        return pltpu.make_async_remote_copy(
            src_ref=ext.at[pl.ds(block_rows, H)], dst_ref=low, send_sem=halo_send.at[0], recv_sem=halo_recv.at[0],
            device_id=coords(lax.rem(me + 1, n)), device_id_type=MESH)

    def to_before():
        return pltpu.make_async_remote_copy(
            src_ref=ext.at[pl.ds(H, H)], dst_ref=high, send_sem=halo_send.at[1], recv_sem=halo_recv.at[1],
            device_id=coords(lax.rem(me + n - 1, n)), device_id_type=MESH)

    @pl.when(me < last)
    def _():
        to_next().start()

    @pl.when(me > 0)
    def _():
        to_before().start()


    @pl.when(me == 0)
    def _():
        low[...] = jnp.zeros_like(low)

    @pl.when(me == last)
    def _():
        high[...] = jnp.zeros_like(high)

    for s in range(3):
        for i in range(half):
            both[0, s:s + 1, i * lanes:(i + 1) * lanes] = planes[s][i:i + 1]
    cov_copy.wait()

    def apply(b):
        acc = jnp.zeros((8, cb), F32)
        for j in range(taps):
            acc = acc + mm_nt(ext[b + H + band[j, b]].astype(BF16), cov[b, j])
        both[1, :, b * cb:(b + 1) * cb] = acc[0:3]

    for b in range(H, block_rows - H):
        apply(b)
    @pl.when(me < last)
    def _():
        to_next().wait_send()
        to_before().wait_recv()

    @pl.when(me > 0)
    def _():
        to_before().wait_send()
        to_next().wait_recv()

    ext[0:H] = low[...]
    ext[block_rows + H:block_rows + 2 * H] = high[...]
    for b in (*range(H), *range(block_rows - H, block_rows)):
        apply(b)
    sent = pl.ds(0, n - 1)
    pltpu.make_async_copy(send.at[sent], send.at[sent], send_sem).wait()


def per_device(n_det, n_tm, timestream, angles, det_weight, pointing, owner, sub_block, cov, band):
    n = n_det * n_tm
    tile_count, pix, length = pointing.shape
    cap = 2 * tile_count // n
    rows = max(16, 2 * cap)
    lanes = 2 * pix
    block_rows, taps, cb, _ = cov.shape
    groups = tile_count // 16
    pixels = block_rows * cb
    hbm = pl.BlockSpec(memory_space=pltpu.HBM)
    both = pl.pallas_call(
        functools.partial(kernel, n_det, n_tm, cap, rows),
        out_shape=pltpu.VMEM((2, 3, pixels), F32),
        in_specs=[hbm] * 8,
        out_specs=pl.BlockSpec(memory_space=pltpu.VMEM),
        scratch_shapes=[
            pltpu.VMEM((1, angles.shape[0]), F32),
            pltpu.VMEM((1, angles.shape[0]), F32),
            pltpu.VMEM((1, tile_count), I32),
            pltpu.VMEM((1, tile_count), I32),
            pltpu.SMEM((taps, block_rows), I32),
            pltpu.VMEM(timestream.shape, BF16),
            pltpu.VMEM(pointing.shape, BF16),
            pltpu.VMEM(cov.shape, BF16),
            pltpu.VMEM((4 * tile_count, length), BF16),
            pltpu.VMEM((2 * tile_count, lanes), F32),
            pltpu.VMEM((n * rows, 2 * tile_count), BF16),
            pltpu.VMEM((n, rows, lanes), BF16),
            pltpu.VMEM((n, rows, lanes), BF16),
            pltpu.VMEM((block_rows + 2 * H, 8, cb), F32),
            pltpu.VMEM((H, 8, cb), F32),
            pltpu.VMEM((H, 8, cb), F32),
            pltpu.SemaphoreType.DMA((5,)),
            pltpu.SemaphoreType.DMA((groups,)),
            pltpu.SemaphoreType.DMA((groups,)),
            pltpu.SemaphoreType.DMA,
            pltpu.SemaphoreType.DMA,
            pltpu.SemaphoreType.DMA,
            pltpu.SemaphoreType.DMA((2,)),
            pltpu.SemaphoreType.DMA((2,)),
        ],
        compiler_params=pltpu.CompilerParams(
            collective_id=0, has_side_effects=True, vmem_limit_bytes=40 * 2**20
        ),
    )(
        *(pltpu.with_memory_space_constraint(x, pltpu.HBM) for x in (
            angles.reshape(1, -1), det_weight.reshape(1, -1), owner.reshape(1, -1), sub_block, band.T,
            timestream, pointing, cov,
        ))
    )
    return both[0], both[1]


def solution(mesh):
    in_specs = (
        P("det", "tm"),
        P("det"),
        P("det"),
        P("tm", None, None),
        P("det", "tm", None),
        P("det", "tm"),
        P(("det", "tm"), None, None, None),
        P(("det", "tm"), None),
    )
    out_specs = (P(None, ("det", "tm")), P(None, ("det", "tm")))
    return jax.shard_map(
        functools.partial(per_device, mesh.shape["det"], mesh.shape["tm"]),
        mesh=mesh, in_specs=in_specs, out_specs=out_specs, check_vma=False,
    )
```

```python
import functools

import jax
import jax.numpy as jnp
from jax import lax
from jax.experimental import pallas as pl
from jax.experimental.pallas import tpu as pltpu
from jax.sharding import PartitionSpec as P

H = 2
MESH = pl.DeviceIdType.MESH
NT = (((1,), (1,)), ((), ()))
F32 = jnp.float32
BF16 = jnp.bfloat16
I32 = jnp.int32


def iota(shape, dim):
    return lax.broadcasted_iota(I32, shape, dim)


def mm(a, b):
    return jnp.dot(a, b, preferred_element_type=F32)


def mm_nt(a, b):
    return lax.dot_general(a, b, NT, preferred_element_type=F32)


def kernel(
    n_det, n_tm, slots,
    angles_hbm, weight_hbm, owner_hbm, sub_hbm, band_hbm, ts_hbm, pt_hbm, cov_hbm,
    both,
    angles, weight, owner, sub, band,
    ts, pt, cov, diag, proj, goal, tiles, pick, note, notes, hits, send, recv, ext, low, high,
    small_sem, ts_sem, pt_sem, cov_sem, note_send, note_recv, send_sem, recv_sem, halo_send, halo_recv,
):
    n = n_det * n_tm
    tile_count = pt.shape[0]
    bounds = tuple(range(0, tile_count + 1, 16))
    stages = len(bounds) - 1
    pix = pt.shape[1]
    length = pt.shape[2]
    lanes = 2 * pix
    me = lax.axis_index("det") * n_tm + lax.axis_index("tm")

    def coords(d):
        return (d // n_tm, d % n_tm)

    small = [
        pltpu.make_async_copy(a, b, small_sem.at[i])
        for i, (a, b) in enumerate((
            (angles_hbm, angles), (weight_hbm, weight), (owner_hbm, owner), (sub_hbm, sub), (band_hbm, band),
        ))
    ]
    for copy in small[:2]:
        copy.start()

    half = tile_count // 2

    def ts_copy(t):
        span = pl.ds(t * length, half * length)
        return pltpu.make_async_copy(ts_hbm.at[:, span], ts.at[:, span], ts_sem.at[t // half])

    def pt_copy(g):
        part = pl.ds(bounds[g], bounds[g + 1] - bounds[g])
        return pltpu.make_async_copy(pt_hbm.at[part], pt.at[part], pt_sem.at[g])

    cov_copy = pltpu.make_async_copy(cov_hbm, cov, cov_sem)
    ts_copy(0).start()
    pt_copy(0).start()
    ts_copy(half).start()
    for copy in small[2:]:
        copy.start()
    barrier = pltpu.get_barrier_semaphore()
    with jax.named_scope("greet"):
        for d in range(n):
            @pl.when(me != d)
            def _():
                pl.semaphore_signal(barrier, inc=1, device_id=(d // n_tm, d % n_tm), device_id_type=MESH)
    with jax.named_scope("small_wait"):
        for copy in small[:2]:
            copy.wait()

    for g in range(1, stages):
        pt_copy(g).start()
    cov_copy.start()
    scope = jax.named_scope("prologue")
    scope.__enter__()
    row8 = iota((8, 8), 0)
    ang = jnp.broadcast_to(2.0 * angles[...], (8, 8))
    wgt = jnp.broadcast_to(weight[...], (8, 8))
    trig = jnp.where(row8 == 0, 1.0, jnp.where(row8 == 1, jnp.cos(ang), jnp.sin(ang)))
    polar = jnp.where(row8 < 3, wgt * trig, 0.0).astype(BF16)
    r = iota((64, 8), 0)
    stokes = jnp.where(r % 2 == 1, 2, (r // 8) % 2)
    spread = mm((stokes == iota((64, 8), 1)).astype(F32).astype(BF16), polar).astype(BF16)
    spread = mm(spread, (iota((8, 128), 1) % 8 == iota((8, 128), 0)).astype(F32).astype(BF16))
    r = iota((64, 128), 0)
    tile_of = 4 * (r // 16) + (r // 2) % 4
    diag[...] = jnp.where(iota((64, 128), 1) // 8 == tile_of, spread, 0.0).astype(BF16)

    def project(low_t, high_t):
        for t in range(low_t, high_t, 16):
            stream = jnp.concatenate(
                [ts[:, k * length:(k + 1) * length].astype(F32) for k in range(t, t + 16)], axis=0
            ).astype(BF16)
            proj[4 * t:4 * t + 64, :] = mm(diag[...], stream).astype(BF16)

    def assign():
        for copy in small[2:4]:
            copy.wait()
        square = (tile_count, tile_count)
        dest = jnp.broadcast_to(owner[...].astype(F32), square)
        dest_column = mm_nt((iota(square, 0) == iota(square, 1)).astype(BF16), dest.astype(BF16))
        earlier = iota(square, 0) < iota(square, 1)
        rank = jnp.sum(jnp.where(earlier & (dest_column == dest), 1.0, 0.0), axis=0, keepdims=True)
        twice = (iota((tile_count, 2 * tile_count), 1) // 2 == iota((tile_count, 2 * tile_count), 0)).astype(BF16)
        pair = jnp.where(iota((8, tile_count), 0) == 0, dest[0:8], jnp.broadcast_to(rank, (8, tile_count)))
        pair = mm(pair.astype(BF16), twice).astype(I32)
        place = pair[0:1] * slots
        turn = pair[1:2]
        both_halves = n * slots + place + turn // 2 + (turn % 2) * (slots // 2)
        odd = iota((1, 2 * tile_count), 1) % 2 == 1
        goal[...] = jnp.broadcast_to(jnp.where(odd, both_halves, place + turn), (8, 2 * tile_count))
        mine = jnp.where(iota((lanes, tile_count), 0) == rank.astype(I32),
                         jnp.broadcast_to(sub[...].astype(F32), (lanes, tile_count)), 0.0).astype(BF16)
        named = (iota((n, tile_count), 0) == owner[...]).astype(F32).astype(BF16)
        note[...] = mm_nt(named, mine).reshape(n, 1, lanes)

    chunk = 2 * n * slots // n_det

    def fill(c):
        pick[c * chunk:(c + 1) * chunk, :] = (
            iota((chunk, 2 * tile_count), 0) + c * chunk == goal[0:1]).astype(F32).astype(BF16)

    ts_copy(0).wait()
    project(0, half)
    scope.__exit__(None, None, None)

    row = iota((8, lanes), 0)
    left = iota((8, lanes), 1) < pix

    pending = []

    def settle(depth):
        while len(pending) > depth:
            t, out = pending.pop(0)
            even = jnp.where(row < 4, out[0:8, 0:lanes], out[0:8, lanes:])
            odds = jnp.where(row < 4, out[8:16, 0:lanes], out[8:16, lanes:])
            first = jnp.where(left, even, pltpu.roll(odds, pix, 1))
            second = jnp.where(left, pltpu.roll(even, pix, 1), odds)
            tiles[2 * t:2 * t + 8, :] = jnp.where((row // 2) % 2 == 0, first, second)

    def tile_maps(g):
        for t in range(bounds[g], bounds[g + 1], 4):
            pending.append((t, mm_nt(proj[4 * t:4 * t + 16, :], pt[t:t + 4].reshape(4 * pix, length))))
            settle(2)

    def to_all(src, dst, sends, arrivals, which):
        for d in which:
            @pl.when(me != d)
            def _():
                pltpu.make_async_remote_copy(
                    src_ref=src.at[d], dst_ref=dst.at[me], send_sem=sends, recv_sem=arrivals,
                    device_id=(d // n_tm, d % n_tm), device_id_type=MESH,
                ).start()

    for g in range(stages):
        with jax.named_scope("stage%d" % g):
            if g == 1:
                ts_copy(half).wait()
                project(half, tile_count)
            if g == stages - 3:
                assign()
            if g == stages - 2:
                pl.semaphore_wait(barrier, n - 1)
                to_all(note, notes, note_send, note_recv, range(n))
            pt_copy(g).wait()
            if g == stages - 2:
                for c in range(n_det):
                    fill(c)
            tile_maps(g)
    settle(0)

    payload = tiles[...].astype(BF16)
    per_z = n // n_det
    part = per_z * slots
    side = iota((per_z, slots // 2, lanes), 2) < pix
    for c in range(n_det):
        choice = jnp.concatenate(
            [pick[c * part:(c + 1) * part, :], pick[n * slots + c * part:n * slots + (c + 1) * part, :]], axis=0)
        out = mm(choice, payload)
        here = slice(c * per_z, (c + 1) * per_z)
        send[here, 0:slots, :] = out[:part].reshape(per_z, slots, lanes).astype(BF16)
        last_rows = out[part:].reshape(per_z, slots, lanes)
        send[here, slots:, :] = jnp.where(side, last_rows[:, :slots // 2], last_rows[:, slots // 2:]).astype(BF16)
        to_all(send, recv, send_sem, recv_sem, range(c * per_z, (c + 1) * per_z))

    notes[me] = note[me]
    recv[me] = send[me]
    ext[...] = jnp.zeros_like(ext)
    others = pl.ds(0, n - 1)
    pltpu.make_async_copy(notes.at[others], notes.at[others], note_recv).wait()
    own_blocks = both.shape[2] // pix
    hb = own_blocks // 2
    entries = n * slots
    entry = iota((lanes, 3 * entries), 1)
    kind = entry // entries
    turn = entry % slots
    from_turn = jnp.where(kind == 0, turn, 2 * turn + kind - 1)
    spread = ((iota((lanes, 3 * entries), 0) == from_turn) & ((kind == 0) | (turn < slots // 2)))
    told = mm(notes[...].reshape(n, lanes).astype(BF16), spread.astype(F32).astype(BF16))
    r = iota((n, 3 * entries), 1)
    told = jnp.sum(jnp.where(iota((n, 3 * entries), 0) == (r % entries) // slots, told, 0.0), axis=0, keepdims=True)
    told = told.astype(I32)
    r = iota((own_blocks, entries), 0)
    wanted = 2 * (r % hb) + r // hb
    for k in range(3):
        hits[k * own_blocks:(k + 1) * own_blocks, :] = (
            wanted == told[:, k * entries:(k + 1) * entries]).astype(F32).astype(BF16)
    pltpu.make_async_copy(recv.at[others], recv.at[others], recv_sem).wait()

    got = recv[...].astype(F32)
    pairs = got[:, 0:slots].reshape(entries, lanes).astype(BF16)
    rest = jnp.concatenate([got[:, slots:], jnp.zeros((n, slots // 2, lanes), F32)], axis=1)
    rest = rest.reshape(entries, lanes).astype(BF16)
    total = mm(hits[0:own_blocks, :], pairs)
    third = mm(hits[own_blocks:, :], rest)
    side = iota((hb, lanes), 1) < pix
    a0, a1 = total[0:hb], total[hb:]
    l0, l1, r0, r1 = (third[hb * i:hb * (i + 1)] for i in range(4))
    planes = (
        jnp.where(side, a0, pltpu.roll(a1, pix, 1)),
        jnp.where(side, pltpu.roll(a0, pix, 1), a1),
        jnp.where(side, l0, r1) + pltpu.roll(jnp.where(side, l1, r0), pix, 1),
    )
    block_rows, taps, cb = cov.shape[0], cov.shape[1], cov.shape[2]
    per = cb // lanes

    def lay(pieces):
        for s in range(3):
            rounded = planes[s].astype(BF16).astype(F32)
            for i in pieces:
                ext[H + i // per, s:s + 1, (i % per) * lanes:(i % per + 1) * lanes] = rounded[i:i + 1]

    lay((*range(H * per), *range(hb - H * per, hb)))
    last = n - 1

    def to_next():
        return pltpu.make_async_remote_copy(
            src_ref=ext.at[pl.ds(block_rows, H)], dst_ref=low, send_sem=halo_send.at[0], recv_sem=halo_recv.at[0],
            device_id=coords(lax.rem(me + 1, n)), device_id_type=MESH)

    def to_before():
        return pltpu.make_async_remote_copy(
            src_ref=ext.at[pl.ds(H, H)], dst_ref=high, send_sem=halo_send.at[1], recv_sem=halo_recv.at[1],
            device_id=coords(lax.rem(me + n - 1, n)), device_id_type=MESH)

    @pl.when(me < last)
    def _():
        to_next().start()

    @pl.when(me > 0)
    def _():
        to_before().start()


    @pl.when(me == 0)
    def _():
        low[...] = jnp.zeros_like(low)

    @pl.when(me == last)
    def _():
        high[...] = jnp.zeros_like(high)

    lay(range(H * per, hb - H * per))
    for s in range(3):
        for i in range(hb):
            both[0, s:s + 1, i * lanes:(i + 1) * lanes] = planes[s][i:i + 1]
    small[4].wait()
    cov_copy.wait()

    def apply(b):
        acc = jnp.zeros((8, cb), F32)
        for j in range(taps):
            acc = acc + mm_nt(ext[b + H + band[j, b]].astype(BF16), cov[b, j])
        both[1, :, b * cb:(b + 1) * cb] = acc[0:3]

    for b in range(H, block_rows - H):
        apply(b)
    @pl.when(me < last)
    def _():
        to_next().wait_send()
        to_before().wait_recv()

    @pl.when(me > 0)
    def _():
        to_before().wait_send()
        to_next().wait_recv()

    ext[0:H] = low[...]
    ext[block_rows + H:block_rows + 2 * H] = high[...]
    for b in (*range(H), *range(block_rows - H, block_rows)):
        apply(b)
    sent = pl.ds(0, n - 1)
    pltpu.make_async_copy(note.at[sent], note.at[sent], note_send).wait()
    pltpu.make_async_copy(send.at[sent], send.at[sent], send_sem).wait()


def per_device(n_det, n_tm, timestream, angles, det_weight, pointing, owner, sub_block, cov, band):
    n = n_det * n_tm
    tile_count, pix, length = pointing.shape
    slots = -(-2 * tile_count // (8 * n)) * 8
    lanes = 2 * pix
    block_rows, taps, cb, _ = cov.shape
    groups = tile_count // 16
    pixels = block_rows * cb
    hbm = pl.BlockSpec(memory_space=pltpu.HBM)
    both = pl.pallas_call(
        functools.partial(kernel, n_det, n_tm, slots),
        out_shape=pltpu.VMEM((2, 3, pixels), F32),
        in_specs=[hbm] * 8,
        out_specs=pl.BlockSpec(memory_space=pltpu.VMEM),
        scratch_shapes=[
            pltpu.VMEM((1, angles.shape[0]), F32),
            pltpu.VMEM((1, angles.shape[0]), F32),
            pltpu.VMEM((1, tile_count), I32),
            pltpu.VMEM((1, tile_count), I32),
            pltpu.SMEM((taps, block_rows), I32),
            pltpu.VMEM(timestream.shape, BF16),
            pltpu.VMEM(pointing.shape, BF16),
            pltpu.VMEM(cov.shape, BF16),
            pltpu.VMEM((64, 128), BF16),
            pltpu.VMEM((4 * tile_count, length), BF16),
            pltpu.VMEM((8, 2 * tile_count), I32),
            pltpu.VMEM((2 * tile_count, lanes), F32),
            pltpu.VMEM((2 * n * slots, 2 * tile_count), BF16),
            pltpu.VMEM((n, 1, lanes), F32),
            pltpu.VMEM((n, 1, lanes), F32),
            pltpu.VMEM((3 * pixels // pix, n * slots), BF16),
            pltpu.VMEM((n, slots + slots // 2, lanes), BF16),
            pltpu.VMEM((n, slots + slots // 2, lanes), BF16),
            pltpu.VMEM((block_rows + 2 * H, 8, cb), F32),
            pltpu.VMEM((H, 8, cb), F32),
            pltpu.VMEM((H, 8, cb), F32),
            pltpu.SemaphoreType.DMA((5,)),
            pltpu.SemaphoreType.DMA((2,)),
            pltpu.SemaphoreType.DMA((groups,)),
            pltpu.SemaphoreType.DMA,
            pltpu.SemaphoreType.DMA,
            pltpu.SemaphoreType.DMA,
            pltpu.SemaphoreType.DMA,
            pltpu.SemaphoreType.DMA,
            pltpu.SemaphoreType.DMA((2,)),
            pltpu.SemaphoreType.DMA((2,)),
        ],
        compiler_params=pltpu.CompilerParams(
            collective_id=0, has_side_effects=True, vmem_limit_bytes=40 * 2**20
        ),
    )(
        *(pltpu.with_memory_space_constraint(x, pltpu.HBM) for x in (
            angles.reshape(1, -1), det_weight.reshape(1, -1), owner.reshape(1, -1), sub_block, band.T,
            timestream, pointing, cov,
        ))
    )
    return both[0], both[1]


def solution(mesh):
    in_specs = (
        P("det", "tm"),
        P("det"),
        P("det"),
        P("tm", None, None),
        P("det", "tm", None),
        P("det", "tm"),
        P(("det", "tm"), None, None, None),
        P(("det", "tm"), None),
    )
    out_specs = (P(None, ("det", "tm")), P(None, ("det", "tm")))
    return jax.shard_map(
        functools.partial(per_device, mesh.shape["det"], mesh.shape["tm"]),
        mesh=mesh, in_specs=in_specs, out_specs=out_specs, check_vma=False,
    )
```

```python
import functools

import jax
import jax.numpy as jnp
from jax import lax
from jax.experimental import pallas as pl
from jax.experimental.pallas import tpu as pltpu
from jax.sharding import PartitionSpec as P

H = 2
MESH = pl.DeviceIdType.MESH
NT = (((1,), (1,)), ((), ()))
F32 = jnp.float32
BF16 = jnp.bfloat16
I32 = jnp.int32


def iota(shape, dim):
    return lax.broadcasted_iota(I32, shape, dim)


def mm(a, b):
    return jnp.dot(a, b, preferred_element_type=F32)


def mm_nt(a, b):
    return lax.dot_general(a, b, NT, preferred_element_type=F32)


def kernel(
    n_det, n_tm, slots,
    angles_hbm, weight_hbm, owner_hbm, sub_hbm, band_hbm, ts_hbm, pt_hbm, cov_hbm,
    both,
    angles, weight, owner, sub, band,
    ts, pt, cov, diag, proj, goal, tiles, pick, note, notes, hits, turned, send, recv, ext, low, high,
    small_sem, ts_sem, pt_sem, cov_sem, note_send, note_recv, send_sem, recv_sem, halo_send, halo_recv,
):
    n = n_det * n_tm
    tile_count = pt.shape[0]
    bounds = tuple(range(0, tile_count + 1, 16))
    stages = len(bounds) - 1
    pix = pt.shape[1]
    length = pt.shape[2]
    lanes = 2 * pix
    me = lax.axis_index("det") * n_tm + lax.axis_index("tm")

    def coords(d):
        return (d // n_tm, d % n_tm)

    small = [
        pltpu.make_async_copy(a, b, small_sem.at[i])
        for i, (a, b) in enumerate((
            (angles_hbm, angles), (weight_hbm, weight), (owner_hbm, owner), (sub_hbm, sub), (band_hbm, band),
        ))
    ]
    for copy in small[:2]:
        copy.start()

    half = tile_count // 2

    def ts_copy(t):
        span = pl.ds(t * length, half * length)
        return pltpu.make_async_copy(ts_hbm.at[:, span], ts.at[:, span], ts_sem.at[t // half])

    def pt_copy(g):
        part = pl.ds(bounds[g], bounds[g + 1] - bounds[g])
        return pltpu.make_async_copy(pt_hbm.at[part], pt.at[part], pt_sem.at[g])

    cov_copy = pltpu.make_async_copy(cov_hbm, cov, cov_sem)
    ts_copy(0).start()
    pt_copy(0).start()
    ts_copy(half).start()
    for copy in small[2:]:
        copy.start()
    barrier = pltpu.get_barrier_semaphore()
    with jax.named_scope("greet"):
        for d in range(n):
            @pl.when(me != d)
            def _():
                pl.semaphore_signal(barrier, inc=1, device_id=(d // n_tm, d % n_tm), device_id_type=MESH)
    with jax.named_scope("small_wait"):
        for copy in small[:2]:
            copy.wait()

    for g in range(1, stages):
        pt_copy(g).start()
    cov_copy.start()
    scope = jax.named_scope("prologue")
    scope.__enter__()
    row8 = iota((8, 8), 0)
    ang = jnp.broadcast_to(2.0 * angles[...], (8, 8))
    wgt = jnp.broadcast_to(weight[...], (8, 8))
    trig = jnp.where(row8 == 0, 1.0, jnp.where(row8 == 1, jnp.cos(ang), jnp.sin(ang)))
    polar = jnp.where(row8 < 3, wgt * trig, 0.0).astype(BF16)
    r = iota((64, 8), 0)
    stokes = jnp.where(r % 2 == 1, 2, (r // 8) % 2)
    spread = mm((stokes == iota((64, 8), 1)).astype(F32).astype(BF16), polar).astype(BF16)
    spread = mm(spread, (iota((8, 128), 1) % 8 == iota((8, 128), 0)).astype(F32).astype(BF16))
    r = iota((64, 128), 0)
    tile_of = 4 * (r // 16) + (r // 2) % 4
    diag[...] = jnp.where(iota((64, 128), 1) // 8 == tile_of, spread, 0.0).astype(BF16)

    def project(low_t, high_t):
        for t in range(low_t, high_t, 16):
            stream = jnp.concatenate(
                [ts[:, k * length:(k + 1) * length].astype(F32) for k in range(t, t + 16)], axis=0
            ).astype(BF16)
            proj[4 * t:4 * t + 64, :] = mm(diag[...], stream).astype(BF16)

    def assign():
        square = (tile_count, tile_count)
        dest = jnp.broadcast_to(owner[...].astype(F32), square)
        dest_column = mm_nt((iota(square, 0) == iota(square, 1)).astype(BF16), dest.astype(BF16))
        earlier = iota(square, 0) < iota(square, 1)
        rank = jnp.sum(jnp.where(earlier & (dest_column == dest), 1.0, 0.0), axis=0, keepdims=True)
        twice = (iota((tile_count, 2 * tile_count), 1) // 2 == iota((tile_count, 2 * tile_count), 0)).astype(BF16)
        pair = jnp.where(iota((8, tile_count), 0) == 0, dest[0:8], jnp.broadcast_to(rank, (8, tile_count)))
        pair = mm(pair.astype(BF16), twice).astype(I32)
        place = pair[0:1] * slots
        turn = pair[1:2]
        both_halves = n * slots + place + turn // 2 + (turn % 2) * (slots // 2)
        odd = iota((1, 2 * tile_count), 1) % 2 == 1
        goal[...] = jnp.broadcast_to(jnp.where(odd, both_halves, place + turn), (8, 2 * tile_count))
        mine = jnp.where(iota((lanes, tile_count), 0) == rank.astype(I32),
                         jnp.broadcast_to(sub[...].astype(F32), (lanes, tile_count)), 0.0).astype(BF16)
        named = (iota((n, tile_count), 0) == owner[...]).astype(F32).astype(BF16)
        note[...] = mm_nt(named, mine).reshape(n, 1, lanes)

    chunk = 2 * n * slots // n_det

    def fill(c):
        pick[c * chunk:(c + 1) * chunk, :] = (
            iota((chunk, 2 * tile_count), 0) + c * chunk == goal[0:1]).astype(F32).astype(BF16)

    ts_copy(0).wait()
    project(0, half)
    scope.__exit__(None, None, None)

    row = iota((8, lanes), 0)
    left = iota((8, lanes), 1) < pix

    pending = []

    def settle(depth):
        while len(pending) > depth:
            t, out = pending.pop(0)
            even = jnp.where(row < 4, out[0:8, 0:lanes], out[0:8, lanes:])
            odds = jnp.where(row < 4, out[8:16, 0:lanes], out[8:16, lanes:])
            first = jnp.where(left, even, pltpu.roll(odds, pix, 1))
            second = jnp.where(left, pltpu.roll(even, pix, 1), odds)
            tiles[2 * t:2 * t + 8, :] = jnp.where((row // 2) % 2 == 0, first, second)

    def tile_maps(g):
        for t in range(bounds[g], bounds[g + 1], 4):
            pending.append((t, mm_nt(proj[4 * t:4 * t + 16, :], pt[t:t + 4].reshape(4 * pix, length))))
            settle(2)

    def to_plane(src, dst, sends, arrivals, z):
        for t in (*range(2, n_tm, 2), 1, 0, *range(3, n_tm, 2)):
            d = z * n_tm + t

            @pl.when(me != d)
            def _():
                pltpu.make_async_remote_copy(
                    src_ref=src.at[d], dst_ref=dst.at[me], send_sem=sends, recv_sem=arrivals,
                    device_id=(z, t), device_id_type=MESH,
                ).start()

    for g in range(stages):
        with jax.named_scope("stage%d" % g):
            if g == 1:
                ts_copy(half).wait()
                project(half, tile_count)
            if g == stages - 3:
                for copy in small[2:4]:
                    copy.wait()
            if g == stages - 2:
                pl.semaphore_wait(barrier, n - 1)
                for z in range(n_det):
                    to_plane(note, notes, note_send, note_recv, z)
            pt_copy(g).wait()
            if g == stages - 3:
                assign()
            if g == stages - 2:
                for c in range(n_det):
                    fill(c)
            tile_maps(g)
    settle(0)

    payload = tiles[...].astype(BF16)
    part = n_tm * slots
    side = iota((n_tm, slots // 2, lanes), 2) < pix
    for z in range(n_det):
        choice = jnp.concatenate(
            [pick[z * part:(z + 1) * part, :], pick[n * slots + z * part:n * slots + (z + 1) * part, :]], axis=0)
        out = mm(choice, payload)
        here = slice(z * n_tm, (z + 1) * n_tm)
        send[here, 0:slots, :] = out[:part].reshape(n_tm, slots, lanes).astype(BF16)
        last_rows = out[part:].reshape(n_tm, slots, lanes)
        send[here, slots:, :] = jnp.where(side, last_rows[:, :slots // 2], last_rows[:, slots // 2:]).astype(BF16)
        to_plane(send, recv, send_sem, recv_sem, z)

    notes[me] = note[me]
    recv[me] = send[me]
    ext[...] = jnp.zeros_like(ext)
    others = pl.ds(0, n - 1)
    pltpu.make_async_copy(notes.at[others], notes.at[others], note_recv).wait()
    own_blocks = both.shape[2] // pix
    hb = own_blocks // 2
    entries = n * slots
    entry = iota((lanes, 3 * entries), 1)
    kind = entry // entries
    turn = entry % slots
    from_turn = jnp.where(kind == 0, turn, 2 * turn + kind - 1)
    spread = ((iota((lanes, 3 * entries), 0) == from_turn) & ((kind == 0) | (turn < slots // 2)))
    told = mm(notes[...].reshape(n, lanes).astype(BF16), spread.astype(F32).astype(BF16))
    r = iota((n, 3 * entries), 1)
    told = jnp.sum(jnp.where(iota((n, 3 * entries), 0) == (r % entries) // slots, told, 0.0), axis=0, keepdims=True)
    told = told.astype(I32)
    r = iota((own_blocks, entries), 0)
    wanted = 2 * (r % hb) + r // hb
    for k in range(3):
        hits[k * own_blocks:(k + 1) * own_blocks, :] = (
            wanted == told[:, k * entries:(k + 1) * entries]).astype(F32).astype(BF16)
    small[4].wait()
    cov_copy.wait()
    block_rows, taps, cb = cov.shape[0], cov.shape[1], cov.shape[2]
    edges = (*range(H), *range(block_rows - H, block_rows))
    identity = (iota((cb, cb), 0) == iota((cb, cb), 1)).astype(F32).astype(BF16)
    for i, b in enumerate(edges):
        for j in range(taps):
            turned[i * taps + j] = mm_nt(identity, cov[b, j]).astype(BF16)
    pltpu.make_async_copy(recv.at[others], recv.at[others], recv_sem).wait()

    got = recv[...].astype(F32)
    pairs = got[:, 0:slots].reshape(entries, lanes).astype(BF16)
    rest = jnp.concatenate([got[:, slots:], jnp.zeros((n, slots // 2, lanes), F32)], axis=1)
    rest = rest.reshape(entries, lanes).astype(BF16)
    total = mm(hits[0:own_blocks, :], pairs)
    third = mm(hits[own_blocks:, :], rest)
    side = iota((hb, lanes), 1) < pix
    a0, a1 = total[0:hb], total[hb:]
    l0, l1, r0, r1 = (third[hb * i:hb * (i + 1)] for i in range(4))
    planes = (
        jnp.where(side, a0, pltpu.roll(a1, pix, 1)),
        jnp.where(side, pltpu.roll(a0, pix, 1), a1),
        jnp.where(side, l0, r1) + pltpu.roll(jnp.where(side, l1, r0), pix, 1),
    )
    per = cb // lanes

    def lay(pieces):
        for s in range(3):
            rounded = planes[s].astype(BF16).astype(F32)
            for i in pieces:
                ext[H + i // per, s:s + 1, (i % per) * lanes:(i % per + 1) * lanes] = rounded[i:i + 1]

    lay((*range(H * per), *range(hb - H * per, hb)))
    last = n - 1

    def to_next():
        return pltpu.make_async_remote_copy(
            src_ref=ext.at[pl.ds(block_rows, H)], dst_ref=low, send_sem=halo_send.at[0], recv_sem=halo_recv.at[0],
            device_id=coords(lax.rem(me + 1, n)), device_id_type=MESH)

    def to_before():
        return pltpu.make_async_remote_copy(
            src_ref=ext.at[pl.ds(H, H)], dst_ref=high, send_sem=halo_send.at[1], recv_sem=halo_recv.at[1],
            device_id=coords(lax.rem(me + n - 1, n)), device_id_type=MESH)

    @pl.when(me < last)
    def _():
        to_next().start()

    @pl.when(me > 0)
    def _():
        to_before().start()


    @pl.when(me == 0)
    def _():
        low[...] = jnp.zeros_like(low)

    @pl.when(me == last)
    def _():
        high[...] = jnp.zeros_like(high)

    lay(range(H * per, hb - H * per))
    for s in range(3):
        for i in range(hb):
            both[0, s:s + 1, i * lanes:(i + 1) * lanes] = planes[s][i:i + 1]
    def apply(b):
        acc = jnp.zeros((8, cb), F32)
        for j in range(taps):
            acc = acc + mm_nt(ext[b + H + band[j, b]].astype(BF16), cov[b, j])
        both[1, :, b * cb:(b + 1) * cb] = acc[0:3]

    for b in range(H, block_rows - H):
        apply(b)
    @pl.when(me < last)
    def _():
        to_next().wait_send()
        to_before().wait_recv()

    @pl.when(me > 0)
    def _():
        to_before().wait_send()
        to_next().wait_recv()

    ext[0:H] = low[...]
    ext[block_rows + H:block_rows + 2 * H] = high[...]
    for i, b in enumerate(edges):
        acc = jnp.zeros((8, cb), F32)
        for j in range(taps):
            acc = acc + mm(ext[b + H + band[j, b]].astype(BF16), turned[i * taps + j])
        both[1, :, b * cb:(b + 1) * cb] = acc[0:3]
    sent = pl.ds(0, n - 1)
    pltpu.make_async_copy(note.at[sent], note.at[sent], note_send).wait()
    pltpu.make_async_copy(send.at[sent], send.at[sent], send_sem).wait()


def per_device(n_det, n_tm, timestream, angles, det_weight, pointing, owner, sub_block, cov, band):
    n = n_det * n_tm
    tile_count, pix, length = pointing.shape
    slots = -(-2 * tile_count // (8 * n)) * 8
    lanes = 2 * pix
    block_rows, taps, cb, _ = cov.shape
    groups = tile_count // 16
    pixels = block_rows * cb
    hbm = pl.BlockSpec(memory_space=pltpu.HBM)
    both = pl.pallas_call(
        functools.partial(kernel, n_det, n_tm, slots),
        out_shape=pltpu.VMEM((2, 3, pixels), F32),
        in_specs=[hbm] * 8,
        out_specs=pl.BlockSpec(memory_space=pltpu.VMEM),
        scratch_shapes=[
            pltpu.VMEM((1, angles.shape[0]), F32),
            pltpu.VMEM((1, angles.shape[0]), F32),
            pltpu.VMEM((1, tile_count), I32),
            pltpu.VMEM((1, tile_count), I32),
            pltpu.SMEM((taps, block_rows), I32),
            pltpu.VMEM(timestream.shape, BF16),
            pltpu.VMEM(pointing.shape, BF16),
            pltpu.VMEM(cov.shape, BF16),
            pltpu.VMEM((64, 128), BF16),
            pltpu.VMEM((4 * tile_count, length), BF16),
            pltpu.VMEM((8, 2 * tile_count), I32),
            pltpu.VMEM((2 * tile_count, lanes), F32),
            pltpu.VMEM((2 * n * slots, 2 * tile_count), BF16),
            pltpu.VMEM((n, 1, lanes), F32),
            pltpu.VMEM((n, 1, lanes), F32),
            pltpu.VMEM((3 * pixels // pix, n * slots), BF16),
            pltpu.VMEM((2 * H * taps, cb, cb), BF16),
            pltpu.VMEM((n, slots + slots // 2, lanes), BF16),
            pltpu.VMEM((n, slots + slots // 2, lanes), BF16),
            pltpu.VMEM((block_rows + 2 * H, 8, cb), F32),
            pltpu.VMEM((H, 8, cb), F32),
            pltpu.VMEM((H, 8, cb), F32),
            pltpu.SemaphoreType.DMA((5,)),
            pltpu.SemaphoreType.DMA((2,)),
            pltpu.SemaphoreType.DMA((groups,)),
            pltpu.SemaphoreType.DMA,
            pltpu.SemaphoreType.DMA,
            pltpu.SemaphoreType.DMA,
            pltpu.SemaphoreType.DMA,
            pltpu.SemaphoreType.DMA,
            pltpu.SemaphoreType.DMA((2,)),
            pltpu.SemaphoreType.DMA((2,)),
        ],
        compiler_params=pltpu.CompilerParams(
            collective_id=0, has_side_effects=True, vmem_limit_bytes=40 * 2**20
        ),
    )(
        *(pltpu.with_memory_space_constraint(x, pltpu.HBM) for x in (
            angles.reshape(1, -1), det_weight.reshape(1, -1), owner.reshape(1, -1), sub_block, band.T,
            timestream, pointing, cov,
        ))
    )
    return both[0], both[1]


def solution(mesh):
    in_specs = (
        P("det", "tm"),
        P("det"),
        P("det"),
        P("tm", None, None),
        P("det", "tm", None),
        P("det", "tm"),
        P(("det", "tm"), None, None, None),
        P(("det", "tm"), None),
    )
    out_specs = (P(None, ("det", "tm")), P(None, ("det", "tm")))
    return jax.shard_map(
        functools.partial(per_device, mesh.shape["det"], mesh.shape["tm"]),
        mesh=mesh, in_specs=in_specs, out_specs=out_specs, check_vma=False,
    )
```

```python
import functools

import jax
import jax.numpy as jnp
from jax import lax
from jax.experimental import pallas as pl
from jax.experimental.pallas import tpu as pltpu
from jax.sharding import PartitionSpec as P

H = 2
MESH = pl.DeviceIdType.MESH
NT = (((1,), (1,)), ((), ()))
F32 = jnp.float32
BF16 = jnp.bfloat16
I32 = jnp.int32


def iota(shape, dim):
    return lax.broadcasted_iota(I32, shape, dim)


def mm(a, b):
    return jnp.dot(a, b, preferred_element_type=F32)


def mm_nt(a, b):
    return lax.dot_general(a, b, NT, preferred_element_type=F32)


def kernel(
    n_det, n_tm, slots,
    angles_hbm, weight_hbm, owner_hbm, sub_hbm, band_hbm, ts_hbm, pt_hbm, cov_hbm,
    both,
    angles, weight, owner, sub, band,
    ts, pt, cov, diag, proj, goal, tiles, pick, note, notes, hits, turned, send, recv, ext, give, low, high,
    small_sem, ts_sem, pt_sem, cov_sem, note_send, note_recv, send_sem, recv_sem, halo_send, halo_recv,
):
    n = n_det * n_tm
    tile_count = pt.shape[0]
    bounds = tuple(range(0, tile_count + 1, 16))
    stages = len(bounds) - 1
    pix = pt.shape[1]
    length = pt.shape[2]
    lanes = 2 * pix
    me = lax.axis_index("det") * n_tm + lax.axis_index("tm")

    def coords(d):
        return (d // n_tm, d % n_tm)

    small = [
        pltpu.make_async_copy(a, b, small_sem.at[i])
        for i, (a, b) in enumerate((
            (angles_hbm, angles), (weight_hbm, weight), (owner_hbm, owner), (sub_hbm, sub), (band_hbm, band),
        ))
    ]
    for copy in small[:4]:
        copy.start()

    half = tile_count // 2

    def ts_copy(t):
        span = pl.ds(t * length, half * length)
        return pltpu.make_async_copy(ts_hbm.at[:, span], ts.at[:, span], ts_sem.at[t // half])

    def pt_copy(g):
        part = pl.ds(bounds[g], bounds[g + 1] - bounds[g])
        return pltpu.make_async_copy(pt_hbm.at[part], pt.at[part], pt_sem.at[g])

    cov_copy = pltpu.make_async_copy(cov_hbm, cov, cov_sem)
    ts_copy(0).start()
    pt_copy(0).start()
    ts_copy(half).start()
    barrier = pltpu.get_barrier_semaphore()
    with jax.named_scope("greet"):
        for d in range(n):
            @pl.when(me != d)
            def _():
                pl.semaphore_signal(barrier, inc=1, device_id=(d // n_tm, d % n_tm), device_id_type=MESH)
    with jax.named_scope("small_wait"):
        for copy in small[:2]:
            copy.wait()

    scope = jax.named_scope("prologue")
    scope.__enter__()
    row8 = iota((8, 8), 0)
    ang = jnp.broadcast_to(2.0 * angles[...], (8, 8))
    wgt = jnp.broadcast_to(weight[...], (8, 8))
    trig = jnp.where(row8 == 0, 1.0, jnp.where(row8 == 1, jnp.cos(ang), jnp.sin(ang)))
    polar = jnp.where(row8 < 3, wgt * trig, 0.0).astype(BF16)
    r = iota((64, 8), 0)
    stokes = jnp.where(r % 2 == 1, 2, (r // 8) % 2)
    spread = mm((stokes == iota((64, 8), 1)).astype(F32).astype(BF16), polar).astype(BF16)
    spread = mm(spread, (iota((8, 128), 1) % 8 == iota((8, 128), 0)).astype(F32).astype(BF16))
    r = iota((64, 128), 0)
    tile_of = 4 * (r // 16) + (r // 2) % 4
    diag[...] = jnp.where(iota((64, 128), 1) // 8 == tile_of, spread, 0.0).astype(BF16)

    def project(low_t, high_t):
        for t in range(low_t, high_t, 16):
            stream = jnp.concatenate(
                [ts[:, k * length:(k + 1) * length].astype(F32) for k in range(t, t + 16)], axis=0
            ).astype(BF16)
            proj[4 * t:4 * t + 64, :] = mm(diag[...], stream).astype(BF16)

    def assign():
        square = (tile_count, tile_count)
        dest = jnp.broadcast_to(owner[...].astype(F32), square)
        dest_column = mm_nt((iota(square, 0) == iota(square, 1)).astype(BF16), dest.astype(BF16))
        earlier = iota(square, 0) < iota(square, 1)
        rank = jnp.sum(jnp.where(earlier & (dest_column == dest), 1.0, 0.0), axis=0, keepdims=True)
        twice = (iota((tile_count, 2 * tile_count), 1) // 2 == iota((tile_count, 2 * tile_count), 0)).astype(BF16)
        pair = jnp.where(iota((8, tile_count), 0) == 0, dest[0:8], jnp.broadcast_to(rank, (8, tile_count)))
        pair = mm(pair.astype(BF16), twice).astype(I32)
        place = pair[0:1] * slots
        turn = pair[1:2]
        both_halves = n * slots + place + turn // 2 + (turn % 2) * (slots // 2)
        odd = iota((1, 2 * tile_count), 1) % 2 == 1
        goal[...] = jnp.broadcast_to(jnp.where(odd, both_halves, place + turn), (8, 2 * tile_count))
        mine = jnp.where(iota((lanes, tile_count), 0) == rank.astype(I32),
                         jnp.broadcast_to(sub[...].astype(F32), (lanes, tile_count)), 0.0).astype(BF16)
        named = (iota((n, tile_count), 0) == owner[...]).astype(F32).astype(BF16)
        note[...] = mm_nt(named, mine).reshape(n, 1, lanes)

    chunk = 2 * n * slots // n_det

    def fill(c):
        pick[c * chunk:(c + 1) * chunk, :] = (
            iota((chunk, 2 * tile_count), 0) + c * chunk == goal[0:1]).astype(F32).astype(BF16)

    for copy in small[2:4]:
        copy.wait()
    for g in range(1, stages):
        pt_copy(g).start()
    small[4].start()
    cov_copy.start()
    ts_copy(0).wait()
    assign()
    project(0, half)
    scope.__exit__(None, None, None)

    row = iota((8, lanes), 0)
    left = iota((8, lanes), 1) < pix

    pending = []

    def settle(depth):
        while len(pending) > depth:
            t, out = pending.pop(0)
            even = jnp.where(row < 4, out[0:8, 0:lanes], out[0:8, lanes:])
            odds = jnp.where(row < 4, out[8:16, 0:lanes], out[8:16, lanes:])
            first = jnp.where(left, even, pltpu.roll(odds, pix, 1))
            second = jnp.where(left, pltpu.roll(even, pix, 1), odds)
            tiles[2 * t:2 * t + 8, :] = jnp.where((row // 2) % 2 == 0, first, second)

    def tile_maps(g):
        for t in range(bounds[g], bounds[g + 1], 4):
            pending.append((t, mm_nt(proj[4 * t:4 * t + 16, :], pt[t:t + 4].reshape(4 * pix, length))))
            settle(2)

    def to_plane(src, dst, sends, arrivals, z):
        for t in ((*range(0, n_tm, 2), *range(1, n_tm, 2)) if z else (*range(2, n_tm, 2), 1, 0, *range(3, n_tm, 2))):
            d = z * n_tm + t

            @pl.when(me != d)
            def _():
                pltpu.make_async_remote_copy(
                    src_ref=src.at[d], dst_ref=dst.at[me], send_sem=sends, recv_sem=arrivals,
                    device_id=(z, t), device_id_type=MESH,
                ).start()

    for g in range(stages):
        with jax.named_scope("stage%d" % g):
            if g == 1:
                ts_copy(half).wait()
                project(half, tile_count)
            if g == stages - 2:
                pl.semaphore_wait(barrier, n - 1)
                for z in range(n_det):
                    to_plane(note, notes, note_send, note_recv, z)
            pt_copy(g).wait()
            if g == stages - 2:
                for c in range(n_det):
                    fill(c)
            tile_maps(g)
    settle(0)

    payload = tiles[...].astype(BF16)
    block_rows, taps, cb = cov.shape[0], cov.shape[1], cov.shape[2]
    edges = (*range(H), *range(block_rows - H, block_rows))
    identity = (iota((cb, cb), 0) == iota((cb, cb), 1)).astype(F32).astype(BF16)

    def turn(i):
        for j in range(taps):
            turned[i * taps + j] = mm_nt(identity, cov[edges[i], j]).astype(BF16)

    part = n_tm * slots
    side = iota((n_tm, slots // 2, lanes), 2) < pix
    for z in range(n_det):
        choice = jnp.concatenate(
            [pick[z * part:(z + 1) * part, :], pick[n * slots + z * part:n * slots + (z + 1) * part, :]], axis=0)
        out = mm(choice, payload)
        here = slice(z * n_tm, (z + 1) * n_tm)
        send[here, 0:slots, :] = out[:part].reshape(n_tm, slots, lanes).astype(BF16)
        last_rows = out[part:].reshape(n_tm, slots, lanes)
        send[here, slots:, :] = jnp.where(side, last_rows[:, :slots // 2], last_rows[:, slots // 2:]).astype(BF16)
        to_plane(send, recv, send_sem, recv_sem, z)
        if z == 0:
            small[4].wait()
            cov_copy.wait()
        for i in range(2 * H * z // n_det, 2 * H * (z + 1) // n_det):
            turn(i)

    notes[me] = note[me]
    recv[me] = send[me]
    ext[...] = jnp.zeros_like(ext)
    give[...] = jnp.zeros_like(give)
    others = pl.ds(0, n - 1)
    pltpu.make_async_copy(notes.at[others], notes.at[others], note_recv).wait()
    own_blocks = both.shape[2] // pix
    hb = own_blocks // 2
    entries = n * slots
    entry = iota((lanes, 3 * entries), 1)
    kind = entry // entries
    turn = entry % slots
    from_turn = jnp.where(kind == 0, turn, 2 * turn + kind - 1)
    spread = ((iota((lanes, 3 * entries), 0) == from_turn) & ((kind == 0) | (turn < slots // 2)))
    told = mm(notes[...].reshape(n, lanes).astype(BF16), spread.astype(F32).astype(BF16))
    r = iota((n, 3 * entries), 1)
    told = jnp.sum(jnp.where(iota((n, 3 * entries), 0) == (r % entries) // slots, told, 0.0), axis=0, keepdims=True)
    told = told.astype(I32)
    r = iota((own_blocks, entries), 0)
    wanted = 2 * (r % hb) + r // hb
    for k in range(3):
        hits[k * own_blocks:(k + 1) * own_blocks, :] = (
            wanted == told[:, k * entries:(k + 1) * entries]).astype(F32).astype(BF16)
    pltpu.make_async_copy(recv.at[others], recv.at[others], recv_sem).wait()

    got = recv[...].astype(F32)
    pairs = got[:, 0:slots].reshape(entries, lanes).astype(BF16)
    rest = jnp.concatenate([got[:, slots:], jnp.zeros((n, slots // 2, lanes), F32)], axis=1)
    rest = rest.reshape(entries, lanes).astype(BF16)
    total = mm(hits[0:own_blocks, :], pairs)
    third = mm(hits[own_blocks:, :], rest)
    side = iota((hb, lanes), 1) < pix
    a0, a1 = total[0:hb], total[hb:]
    l0, l1, r0, r1 = (third[hb * i:hb * (i + 1)] for i in range(4))
    planes = (
        jnp.where(side, a0, pltpu.roll(a1, pix, 1)),
        jnp.where(side, pltpu.roll(a0, pix, 1), a1),
        jnp.where(side, l0, r1) + pltpu.roll(jnp.where(side, l1, r0), pix, 1),
    )
    per = cb // lanes

    rounded = [plane.astype(BF16).astype(F32) for plane in planes]
    for s in range(3):
        for i in range(H * per):
            at = (slice(4 * (i // per) + s, 4 * (i // per) + s + 1), slice((i % per) * lanes, (i % per + 1) * lanes))
            give[0, at[0], at[1]] = rounded[s][i:i + 1]
            give[1, at[0], at[1]] = rounded[s][hb - H * per + i:hb - H * per + i + 1]

    last = n - 1

    def to_next():
        return pltpu.make_async_remote_copy(
            src_ref=give.at[1], dst_ref=low, send_sem=halo_send.at[0], recv_sem=halo_recv.at[0],
            device_id=coords(lax.rem(me + 1, n)), device_id_type=MESH)

    def to_before():
        return pltpu.make_async_remote_copy(
            src_ref=give.at[0], dst_ref=high, send_sem=halo_send.at[1], recv_sem=halo_recv.at[1],
            device_id=coords(lax.rem(me + n - 1, n)), device_id_type=MESH)

    @pl.when(me < last)
    def _():
        to_next().start()

    @pl.when(me > 0)
    def _():
        to_before().start()


    @pl.when(me == 0)
    def _():
        low[...] = jnp.zeros_like(low)

    @pl.when(me == last)
    def _():
        high[...] = jnp.zeros_like(high)

    for s in range(3):
        for i in range(hb):
            ext[H + i // per, s:s + 1, (i % per) * lanes:(i % per + 1) * lanes] = rounded[s][i:i + 1]
    for s in range(3):
        for i in range(hb):
            both[0, s:s + 1, i * lanes:(i + 1) * lanes] = planes[s][i:i + 1]
    def apply(b):
        acc = jnp.zeros((8, cb), F32)
        for j in range(taps):
            acc = acc + mm_nt(ext[b + H + band[j, b]].astype(BF16), cov[b, j])
        both[1, :, b * cb:(b + 1) * cb] = acc[0:3]

    for b in range(H, block_rows - H):
        apply(b)
    @pl.when(me < last)
    def _():
        to_next().wait_send()
        to_before().wait_recv()

    @pl.when(me > 0)
    def _():
        to_before().wait_send()
        to_next().wait_recv()

    for h in range(H):
        ext[h, 0:3, :] = low[4 * h:4 * h + 3, :]
        ext[block_rows + H + h, 0:3, :] = high[4 * h:4 * h + 3, :]
    for i, b in enumerate(edges):
        acc = jnp.zeros((8, cb), F32)
        for j in range(taps):
            acc = acc + mm(ext[b + H + band[j, b]].astype(BF16), turned[i * taps + j])
        both[1, :, b * cb:(b + 1) * cb] = acc[0:3]
    sent = pl.ds(0, n - 1)
    pltpu.make_async_copy(note.at[sent], note.at[sent], note_send).wait()
    pltpu.make_async_copy(send.at[sent], send.at[sent], send_sem).wait()


def per_device(n_det, n_tm, timestream, angles, det_weight, pointing, owner, sub_block, cov, band):
    n = n_det * n_tm
    tile_count, pix, length = pointing.shape
    slots = -(-2 * tile_count // (8 * n)) * 8
    lanes = 2 * pix
    block_rows, taps, cb, _ = cov.shape
    groups = tile_count // 16
    pixels = block_rows * cb
    hbm = pl.BlockSpec(memory_space=pltpu.HBM)
    both = pl.pallas_call(
        functools.partial(kernel, n_det, n_tm, slots),
        out_shape=pltpu.VMEM((2, 3, pixels), F32),
        in_specs=[hbm] * 8,
        out_specs=pl.BlockSpec(memory_space=pltpu.VMEM),
        scratch_shapes=[
            pltpu.VMEM((1, angles.shape[0]), F32),
            pltpu.VMEM((1, angles.shape[0]), F32),
            pltpu.VMEM((1, tile_count), I32),
            pltpu.VMEM((1, tile_count), I32),
            pltpu.SMEM((taps, block_rows), I32),
            pltpu.VMEM(timestream.shape, BF16),
            pltpu.VMEM(pointing.shape, BF16),
            pltpu.VMEM(cov.shape, BF16),
            pltpu.VMEM((64, 128), BF16),
            pltpu.VMEM((4 * tile_count, length), BF16),
            pltpu.VMEM((8, 2 * tile_count), I32),
            pltpu.VMEM((2 * tile_count, lanes), F32),
            pltpu.VMEM((2 * n * slots, 2 * tile_count), BF16),
            pltpu.VMEM((n, 1, lanes), F32),
            pltpu.VMEM((n, 1, lanes), F32),
            pltpu.VMEM((3 * pixels // pix, n * slots), BF16),
            pltpu.VMEM((2 * H * taps, cb, cb), BF16),
            pltpu.VMEM((n, slots + slots // 2, lanes), BF16),
            pltpu.VMEM((n, slots + slots // 2, lanes), BF16),
            pltpu.VMEM((block_rows + 2 * H, 8, cb), F32),
            pltpu.VMEM((2, 4 * H, cb), F32),
            pltpu.VMEM((4 * H, cb), F32),
            pltpu.VMEM((4 * H, cb), F32),
            pltpu.SemaphoreType.DMA((5,)),
            pltpu.SemaphoreType.DMA((2,)),
            pltpu.SemaphoreType.DMA((groups,)),
            pltpu.SemaphoreType.DMA,
            pltpu.SemaphoreType.DMA,
            pltpu.SemaphoreType.DMA,
            pltpu.SemaphoreType.DMA,
            pltpu.SemaphoreType.DMA,
            pltpu.SemaphoreType.DMA((2,)),
            pltpu.SemaphoreType.DMA((2,)),
        ],
        compiler_params=pltpu.CompilerParams(
            collective_id=0, has_side_effects=True, vmem_limit_bytes=40 * 2**20
        ),
    )(
        *(pltpu.with_memory_space_constraint(x, pltpu.HBM) for x in (
            angles.reshape(1, -1), det_weight.reshape(1, -1), owner.reshape(1, -1), sub_block, band.T,
            timestream, pointing, cov,
        ))
    )
    return both[0], both[1]


def solution(mesh):
    in_specs = (
        P("det", "tm"),
        P("det"),
        P("det"),
        P("tm", None, None),
        P("det", "tm", None),
        P("det", "tm"),
        P(("det", "tm"), None, None, None),
        P(("det", "tm"), None),
    )
    out_specs = (P(None, ("det", "tm")), P(None, ("det", "tm")))
    return jax.shard_map(
        functools.partial(per_device, mesh.shape["det"], mesh.shape["tm"]),
        mesh=mesh, in_specs=in_specs, out_specs=out_specs, check_vma=False,
    )
```

```python
import functools

import jax
import jax.numpy as jnp
from jax import lax
from jax.experimental import pallas as pl
from jax.experimental.pallas import tpu as pltpu
from jax.sharding import PartitionSpec as P

H = 2
MESH = pl.DeviceIdType.MESH
NT = (((1,), (1,)), ((), ()))
F32 = jnp.float32
BF16 = jnp.bfloat16
I32 = jnp.int32


def iota(shape, dim):
    return lax.broadcasted_iota(I32, shape, dim)


def mm(a, b):
    return jnp.dot(a, b, preferred_element_type=F32)


def mm_nt(a, b):
    return lax.dot_general(a, b, NT, preferred_element_type=F32)


def kernel(
    n_det, n_tm, slots,
    angles_hbm, weight_hbm, owner_hbm, sub_hbm, band_hbm, ts_hbm, pt_hbm, cov_hbm,
    both,
    angles, weight, owner, sub, band,
    ts, pt, cov, diag, proj, goal, tiles, pick, note, notes, hits, turned, send, recv, ext, give, halo,
    small_sem, ts_sem, pt_sem, note_recv, recv_sem, halo_recv,
):
    n = n_det * n_tm
    tile_count = pt.shape[0]
    bounds = tuple(range(0, tile_count + 1, 16))
    stages = len(bounds) - 1
    pix = pt.shape[1]
    length = pt.shape[2]
    lanes = 2 * pix
    me = lax.axis_index("det") * n_tm + lax.axis_index("tm")

    def coords(d):
        return (d // n_tm, d % n_tm)

    cov_sem, note_send, send_sem = small_sem.at[0], small_sem.at[1], small_sem.at[2]
    halo_send = (small_sem.at[3], pt_sem.at[0])
    small = [
        pltpu.make_async_copy(a, b, small_sem.at[i])
        for i, (a, b) in enumerate((
            (angles_hbm, angles), (weight_hbm, weight), (owner_hbm, owner), (sub_hbm, sub), (band_hbm, band),
        ))
    ]
    for copy in small[:4]:
        copy.start()

    half = tile_count // 2

    def ts_copy(t):
        span = pl.ds(t * length, half * length)
        return pltpu.make_async_copy(ts_hbm.at[:, span], ts.at[:, span], ts_sem.at[t // half])

    def pt_copy(g):
        part = pl.ds(bounds[g], bounds[g + 1] - bounds[g])
        return pltpu.make_async_copy(pt_hbm.at[part], pt.at[part], pt_sem.at[g])

    cov_copy = pltpu.make_async_copy(cov_hbm, cov, cov_sem)
    ts_copy(0).start()
    pt_copy(0).start()
    ts_copy(half).start()
    barrier = pltpu.get_barrier_semaphore()
    with jax.named_scope("greet"):
        for d in range(n):
            @pl.when(me != d)
            def _():
                pl.semaphore_signal(barrier, inc=1, device_id=(d // n_tm, d % n_tm), device_id_type=MESH)
    with jax.named_scope("small_wait"):
        for copy in small[:2]:
            copy.wait()

    scope = jax.named_scope("prologue")
    scope.__enter__()
    row8 = iota((8, 8), 0)
    ang = jnp.broadcast_to(2.0 * angles[...], (8, 8))
    wgt = jnp.broadcast_to(weight[...], (8, 8))
    trig = jnp.where(row8 == 0, 1.0, jnp.where(row8 == 1, jnp.cos(ang), jnp.sin(ang)))
    polar = jnp.where(row8 < 3, wgt * trig, 0.0).astype(BF16)
    r = iota((64, 8), 0)
    stokes = jnp.where(r % 2 == 1, 2, (r // 8) % 2)
    spread = mm((stokes == iota((64, 8), 1)).astype(F32).astype(BF16), polar).astype(BF16)
    spread = mm(spread, (iota((8, 128), 1) % 8 == iota((8, 128), 0)).astype(F32).astype(BF16))
    r = iota((64, 128), 0)
    tile_of = 4 * (r // 16) + (r // 2) % 4
    diag[...] = jnp.where(iota((64, 128), 1) // 8 == tile_of, spread, 0.0).astype(BF16)

    def project(low_t, high_t):
        for t in range(low_t, high_t, 16):
            stream = jnp.concatenate(
                [ts[:, k * length:(k + 1) * length].astype(F32) for k in range(t, t + 16)], axis=0
            ).astype(BF16)
            proj[4 * t:4 * t + 64, :] = mm(diag[...], stream).astype(BF16)

    def assign():
        square = (tile_count, tile_count)
        dest = jnp.broadcast_to(owner[...].astype(F32), square)
        dest_column = mm_nt((iota(square, 0) == iota(square, 1)).astype(BF16), dest.astype(BF16))
        earlier = iota(square, 0) < iota(square, 1)
        rank = jnp.sum(jnp.where(earlier & (dest_column == dest), 1.0, 0.0), axis=0, keepdims=True)
        twice = (iota((tile_count, 2 * tile_count), 1) // 2 == iota((tile_count, 2 * tile_count), 0)).astype(BF16)
        pair = jnp.where(iota((8, tile_count), 0) == 0, dest[0:8], jnp.broadcast_to(rank, (8, tile_count)))
        pair = mm(pair.astype(BF16), twice).astype(I32)
        place = pair[0:1] * slots
        turn = pair[1:2]
        both_halves = n * slots + place + turn // 2 + (turn % 2) * (slots // 2)
        odd = iota((1, 2 * tile_count), 1) % 2 == 1
        goal[...] = jnp.broadcast_to(jnp.where(odd, both_halves, place + turn), (8, 2 * tile_count))
        mine = jnp.where(iota((lanes, tile_count), 0) == rank.astype(I32),
                         jnp.broadcast_to(sub[...].astype(F32), (lanes, tile_count)), 0.0).astype(BF16)
        named = (iota((n, tile_count), 0) == owner[...]).astype(F32).astype(BF16)
        note[...] = mm_nt(named, mine).reshape(n, 1, lanes)

    chunk = 2 * n * slots // n_det

    def fill(c):
        pick[c * chunk:(c + 1) * chunk, :] = (
            iota((chunk, 2 * tile_count), 0) + c * chunk == goal[0:1]).astype(F32).astype(BF16)

    for copy in small[2:4]:
        copy.wait()
    for g in range(1, stages):
        pt_copy(g).start()
    small[4].start()
    cov_copy.start()
    ts_copy(0).wait()
    assign()
    project(0, half)
    scope.__exit__(None, None, None)

    row = iota((8, lanes), 0)
    left = iota((8, lanes), 1) < pix

    pending = []

    def settle(depth):
        while len(pending) > depth:
            t, out = pending.pop(0)
            even = jnp.where(row < 4, out[0:8, 0:lanes], out[0:8, lanes:])
            odds = jnp.where(row < 4, out[8:16, 0:lanes], out[8:16, lanes:])
            first = jnp.where(left, even, pltpu.roll(odds, pix, 1))
            second = jnp.where(left, pltpu.roll(even, pix, 1), odds)
            tiles[2 * t:2 * t + 8, :] = jnp.where((row // 2) % 2 == 0, first, second)

    def tile_maps(g):
        for t in range(bounds[g], bounds[g + 1], 4):
            pending.append((t, mm_nt(proj[4 * t:4 * t + 16, :], pt[t:t + 4].reshape(4 * pix, length))))
            settle(2)

    def to_plane(src, dst, sends, arrivals, z):
        for t in ((*range(0, n_tm, 2), *range(1, n_tm, 2)) if z else (*range(2, n_tm, 2), 1, 0, *range(3, n_tm, 2))):
            d = z * n_tm + t

            @pl.when(me != d)
            def _():
                pltpu.make_async_remote_copy(
                    src_ref=src.at[d], dst_ref=dst.at[me], send_sem=sends, recv_sem=arrivals,
                    device_id=(z, t), device_id_type=MESH,
                ).start()

    for g in range(stages):
        with jax.named_scope("stage%d" % g):
            if g == 1:
                ts_copy(half).wait()
                project(half, tile_count)
            if g == stages - 2:
                pl.semaphore_wait(barrier, n - 1)
                for z in range(n_det):
                    to_plane(note, notes, note_send, note_recv, z)
            pt_copy(g).wait()
            if g == stages - 2:
                for c in range(n_det):
                    fill(c)
            tile_maps(g)
    settle(0)

    payload = tiles[...].astype(BF16)
    block_rows, taps, cb = cov.shape[0], cov.shape[1], cov.shape[2]
    edges = (*range(H), *range(block_rows - H, block_rows))
    identity = (iota((cb, cb), 0) == iota((cb, cb), 1)).astype(F32).astype(BF16)

    def turn(b):
        for j in range(taps):
            turned[b * taps + j] = mm_nt(identity, cov[b, j]).astype(BF16)

    part = n_tm * slots
    side = iota((n_tm, slots // 2, lanes), 2) < pix
    for z in range(n_det):
        choice = jnp.concatenate(
            [pick[z * part:(z + 1) * part, :], pick[n * slots + z * part:n * slots + (z + 1) * part, :]], axis=0)
        out = mm(choice, payload)
        here = slice(z * n_tm, (z + 1) * n_tm)
        send[here, 0:slots, :] = out[:part].reshape(n_tm, slots, lanes).astype(BF16)
        last_rows = out[part:].reshape(n_tm, slots, lanes)
        send[here, slots:, :] = jnp.where(side, last_rows[:, :slots // 2], last_rows[:, slots // 2:]).astype(BF16)
        to_plane(send, recv, send_sem, recv_sem, z)
        if z == 0:
            small[4].wait()
            cov_copy.wait()
        for i in range(2 * H * z // n_det, 2 * H * (z + 1) // n_det):
            turn(edges[i])
    for b in range(H, block_rows - H):
        turn(b)

    notes[me] = note[me]
    recv[me] = send[me]
    ext[...] = jnp.zeros_like(ext)
    give[...] = jnp.zeros_like(give)
    others = pl.ds(0, n - 1)
    pltpu.make_async_copy(notes.at[others], notes.at[others], note_recv).wait()
    own_blocks = both.shape[2] // pix
    hb = own_blocks // 2
    entries = n * slots
    entry = iota((lanes, 3 * entries), 1)
    kind = entry // entries
    turn = entry % slots
    from_turn = jnp.where(kind == 0, turn, 2 * turn + kind - 1)
    spread = ((iota((lanes, 3 * entries), 0) == from_turn) & ((kind == 0) | (turn < slots // 2)))
    told = mm(notes[...].reshape(n, lanes).astype(BF16), spread.astype(F32).astype(BF16))
    r = iota((n, 3 * entries), 1)
    told = jnp.sum(jnp.where(iota((n, 3 * entries), 0) == (r % entries) // slots, told, 0.0), axis=0, keepdims=True)
    told = told.astype(I32)
    r = iota((own_blocks, entries), 0)
    wanted = 2 * (r % hb) + r // hb
    for k in range(3):
        hits[k * own_blocks:(k + 1) * own_blocks, :] = (
            wanted == told[:, k * entries:(k + 1) * entries]).astype(F32).astype(BF16)
    pltpu.make_async_copy(recv.at[others], recv.at[others], recv_sem).wait()

    got = recv[...].astype(F32)
    pairs = got[:, 0:slots].reshape(entries, lanes).astype(BF16)
    rest = jnp.concatenate([got[:, slots:], jnp.zeros((n, slots // 2, lanes), F32)], axis=1)
    rest = rest.reshape(entries, lanes).astype(BF16)
    total = mm(hits[0:own_blocks, :], pairs)
    third = mm(hits[own_blocks:, :], rest)
    side = iota((hb, lanes), 1) < pix
    a0, a1 = total[0:hb], total[hb:]
    l0, l1, r0, r1 = (third[hb * i:hb * (i + 1)] for i in range(4))
    planes = (
        jnp.where(side, a0, pltpu.roll(a1, pix, 1)),
        jnp.where(side, pltpu.roll(a0, pix, 1), a1),
        jnp.where(side, l0, r1) + pltpu.roll(jnp.where(side, l1, r0), pix, 1),
    )
    per = cb // lanes

    rounded = [plane.astype(BF16).astype(F32) for plane in planes]
    for s in range(3):
        for i in range(H * per):
            at = (slice(4 * (i // per) + s, 4 * (i // per) + s + 1), slice((i % per) * lanes, (i % per + 1) * lanes))
            give[0, at[0], at[1]] = rounded[s][i:i + 1]
            give[1, at[0], at[1]] = rounded[s][hb - H * per + i:hb - H * per + i + 1]

    last = n - 1

    def to_next():
        return pltpu.make_async_remote_copy(
            src_ref=give.at[1], dst_ref=halo.at[0], send_sem=halo_send[0], recv_sem=halo_recv.at[0],
            device_id=coords(lax.rem(me + 1, n)), device_id_type=MESH)

    def to_before():
        return pltpu.make_async_remote_copy(
            src_ref=give.at[0], dst_ref=halo.at[1], send_sem=halo_send[1], recv_sem=halo_recv.at[1],
            device_id=coords(lax.rem(me + n - 1, n)), device_id_type=MESH)

    @pl.when(me < last)
    def _():
        to_next().start()

    @pl.when(me > 0)
    def _():
        to_before().start()


    @pl.when(me == 0)
    def _():
        halo[0] = jnp.zeros(halo.shape[1:], F32)

    @pl.when(me == last)
    def _():
        halo[1] = jnp.zeros(halo.shape[1:], F32)

    for s in range(3):
        for i in range(hb):
            ext[H + i // per, s:s + 1, (i % per) * lanes:(i % per + 1) * lanes] = rounded[s][i:i + 1]
    for s in range(3):
        for i in range(hb):
            both[0, s:s + 1, i * lanes:(i + 1) * lanes] = planes[s][i:i + 1]
    def apply(b, at):
        acc = jnp.zeros((8, cb), F32)
        for j in range(taps):
            acc = acc + mm(ext[b + H + band[j, b]].astype(BF16), turned[b * taps + j])
        both[1, :, at] = acc[0:3]

    for b in range(H, block_rows - H):
        apply(b, slice(b * cb, (b + 1) * cb))

    def finish(k):
        @pl.when(jnp.where(k == 0, me, last - me) > 0)
        def _():
            pltpu.make_async_copy(halo.at[k], halo.at[k], halo_recv.at[k]).wait()

        for h in range(H):
            ext[k * (block_rows + H) + h, 0:3, :] = halo[k, 4 * h:4 * h + 3, :]
        for h in range(H):
            b = k * (block_rows - H) + h
            apply(b, pl.ds(pl.multiple_of(b * cb, cb), cb))

    near = 1 - me % 2
    with jax.named_scope("near"):
        finish(near)
    with jax.named_scope("far"):
        finish(1 - near)

    @pl.when(me < last)
    def _():
        to_next().wait_send()

    @pl.when(me > 0)
    def _():
        to_before().wait_send()

    sent = pl.ds(0, n - 1)
    pltpu.make_async_copy(note.at[sent], note.at[sent], note_send).wait()
    pltpu.make_async_copy(send.at[sent], send.at[sent], send_sem).wait()


def per_device(n_det, n_tm, timestream, angles, det_weight, pointing, owner, sub_block, cov, band):
    n = n_det * n_tm
    tile_count, pix, length = pointing.shape
    slots = -(-2 * tile_count // (8 * n)) * 8
    lanes = 2 * pix
    block_rows, taps, cb, _ = cov.shape
    groups = tile_count // 16
    pixels = block_rows * cb
    hbm = pl.BlockSpec(memory_space=pltpu.HBM)
    both = pl.pallas_call(
        functools.partial(kernel, n_det, n_tm, slots),
        out_shape=pltpu.VMEM((2, 3, pixels), F32),
        in_specs=[hbm] * 8,
        out_specs=pl.BlockSpec(memory_space=pltpu.VMEM),
        scratch_shapes=[
            pltpu.VMEM((1, angles.shape[0]), F32),
            pltpu.VMEM((1, angles.shape[0]), F32),
            pltpu.VMEM((1, tile_count), I32),
            pltpu.VMEM((1, tile_count), I32),
            pltpu.SMEM((taps, block_rows), I32),
            pltpu.VMEM(timestream.shape, BF16),
            pltpu.VMEM(pointing.shape, BF16),
            pltpu.VMEM(cov.shape, BF16),
            pltpu.VMEM((64, 128), BF16),
            pltpu.VMEM((4 * tile_count, length), BF16),
            pltpu.VMEM((8, 2 * tile_count), I32),
            pltpu.VMEM((2 * tile_count, lanes), F32),
            pltpu.VMEM((2 * n * slots, 2 * tile_count), BF16),
            pltpu.VMEM((n, 1, lanes), F32),
            pltpu.VMEM((n, 1, lanes), F32),
            pltpu.VMEM((3 * pixels // pix, n * slots), BF16),
            pltpu.VMEM((block_rows * taps, cb, cb), BF16),
            pltpu.VMEM((n, slots + slots // 2, lanes), BF16),
            pltpu.VMEM((n, slots + slots // 2, lanes), BF16),
            pltpu.VMEM((block_rows + 2 * H, 8, cb), F32),
            pltpu.VMEM((2, 4 * H, cb), F32),
            pltpu.VMEM((2, 4 * H, cb), F32),
            pltpu.SemaphoreType.DMA((5,)),
            pltpu.SemaphoreType.DMA((2,)),
            pltpu.SemaphoreType.DMA((groups,)),
            pltpu.SemaphoreType.DMA,
            pltpu.SemaphoreType.DMA,
            pltpu.SemaphoreType.DMA((2,)),
        ],
        compiler_params=pltpu.CompilerParams(
            collective_id=0, has_side_effects=True, vmem_limit_bytes=40 * 2**20
        ),
    )(
        *(pltpu.with_memory_space_constraint(x, pltpu.HBM) for x in (
            angles.reshape(1, -1), det_weight.reshape(1, -1), owner.reshape(1, -1), sub_block, band.T,
            timestream, pointing, cov,
        ))
    )
    return both[0], both[1]


def solution(mesh):
    in_specs = (
        P("det", "tm"),
        P("det"),
        P("det"),
        P("tm", None, None),
        P("det", "tm", None),
        P("det", "tm"),
        P(("det", "tm"), None, None, None),
        P(("det", "tm"), None),
    )
    out_specs = (P(None, ("det", "tm")), P(None, ("det", "tm")))
    return jax.shard_map(
        functools.partial(per_device, mesh.shape["det"], mesh.shape["tm"]),
        mesh=mesh, in_specs=in_specs, out_specs=out_specs, check_vma=False,
    )
```

```python
import functools

import jax
import jax.numpy as jnp
from jax import lax
from jax.experimental import pallas as pl
from jax.experimental.pallas import tpu as pltpu
from jax.sharding import PartitionSpec as P

H = 2
MESH = pl.DeviceIdType.MESH
NT = (((1,), (1,)), ((), ()))
F32 = jnp.float32
BF16 = jnp.bfloat16
I32 = jnp.int32


def iota(shape, dim):
    return lax.broadcasted_iota(I32, shape, dim)


def mm(a, b):
    return jnp.dot(a, b, preferred_element_type=F32)


def mm_nt(a, b):
    return lax.dot_general(a, b, NT, preferred_element_type=F32)


def kernel(
    n_det, n_tm, slots,
    angles_hbm, weight_hbm, owner_hbm, sub_hbm, band_hbm, ts_hbm, pt_hbm, cov_hbm,
    both,
    angles, weight, owner, sub, band,
    ts, pt, cov, diag, proj, goal, tiles, pick, note, notes, hits, turned, send, recv, ext, give, halo,
    small_sem, ts_sem, pt_sem, note_recv, recv_sem, halo_recv,
):
    n = n_det * n_tm
    tile_count = pt.shape[0]
    bounds = tuple(range(0, tile_count + 1, 16))
    stages = len(bounds) - 1
    pix = pt.shape[1]
    length = pt.shape[2]
    lanes = 2 * pix
    me = lax.axis_index("det") * n_tm + lax.axis_index("tm")

    def coords(d):
        return (d // n_tm, d % n_tm)

    cov_sem, note_send, send_sem = small_sem.at[0], small_sem.at[1], small_sem.at[2]
    halo_send = (small_sem.at[3], pt_sem.at[0])
    small = [
        pltpu.make_async_copy(a, b, small_sem.at[i])
        for i, (a, b) in enumerate((
            (angles_hbm, angles), (weight_hbm, weight), (owner_hbm, owner), (sub_hbm, sub), (band_hbm, band),
        ))
    ]
    for copy in small[:4]:
        copy.start()

    half = tile_count // 2

    def ts_copy(t):
        span = pl.ds(t * length, half * length)
        return pltpu.make_async_copy(ts_hbm.at[:, span], ts.at[:, span], ts_sem.at[t // half])

    def pt_copy(g):
        part = pl.ds(bounds[g], bounds[g + 1] - bounds[g])
        return pltpu.make_async_copy(pt_hbm.at[part], pt.at[part], pt_sem.at[g])

    cov_copy = pltpu.make_async_copy(cov_hbm, cov, cov_sem)
    ts_copy(0).start()
    pt_copy(0).start(priority=1)
    for g in range(1, stages):
        pt_copy(g).start(priority=1)
    barrier = pltpu.get_barrier_semaphore()
    with jax.named_scope("greet"):
        for d in range(n):
            @pl.when(me != d)
            def _():
                pl.semaphore_signal(barrier, inc=1, device_id=(d // n_tm, d % n_tm), device_id_type=MESH)
    with jax.named_scope("small_wait"):
        for copy in small[:2]:
            copy.wait()

    ts_copy(half).start()
    scope = jax.named_scope("prologue")
    scope.__enter__()
    row8 = iota((8, 8), 0)
    ang = jnp.broadcast_to(2.0 * angles[...], (8, 8))
    wgt = jnp.broadcast_to(weight[...], (8, 8))
    trig = jnp.where(row8 == 0, 1.0, jnp.where(row8 == 1, jnp.cos(ang), jnp.sin(ang)))
    polar = jnp.where(row8 < 3, wgt * trig, 0.0).astype(BF16)
    r = iota((64, 8), 0)
    stokes = jnp.where(r % 2 == 1, 2, (r // 8) % 2)
    spread = mm((stokes == iota((64, 8), 1)).astype(F32).astype(BF16), polar).astype(BF16)
    spread = mm(spread, (iota((8, 128), 1) % 8 == iota((8, 128), 0)).astype(F32).astype(BF16))
    r = iota((64, 128), 0)
    tile_of = 4 * (r // 16) + (r // 2) % 4
    diag[...] = jnp.where(iota((64, 128), 1) // 8 == tile_of, spread, 0.0).astype(BF16)

    def project(low_t, high_t):
        for t in range(low_t, high_t, 16):
            stream = jnp.concatenate(
                [ts[:, k * length:(k + 1) * length].astype(F32) for k in range(t, t + 16)], axis=0
            ).astype(BF16)
            proj[4 * t:4 * t + 64, :] = mm(diag[...], stream).astype(BF16)

    def assign():
        square = (tile_count, tile_count)
        dest = jnp.broadcast_to(owner[...].astype(F32), square)
        dest_column = mm_nt((iota(square, 0) == iota(square, 1)).astype(BF16), dest.astype(BF16))
        earlier = iota(square, 0) < iota(square, 1)
        rank = jnp.sum(jnp.where(earlier & (dest_column == dest), 1.0, 0.0), axis=0, keepdims=True)
        twice = (iota((tile_count, 2 * tile_count), 1) // 2 == iota((tile_count, 2 * tile_count), 0)).astype(BF16)
        pair = jnp.where(iota((8, tile_count), 0) == 0, dest[0:8], jnp.broadcast_to(rank, (8, tile_count)))
        pair = mm(pair.astype(BF16), twice).astype(I32)
        place = pair[0:1] * slots
        turn = pair[1:2]
        both_halves = n * slots + place + turn // 2 + (turn % 2) * (slots // 2)
        odd = iota((1, 2 * tile_count), 1) % 2 == 1
        goal[...] = jnp.broadcast_to(jnp.where(odd, both_halves, place + turn), (8, 2 * tile_count))
        mine = jnp.where(iota((lanes, tile_count), 0) == rank.astype(I32),
                         jnp.broadcast_to(sub[...].astype(F32), (lanes, tile_count)), 0.0).astype(BF16)
        named = (iota((n, tile_count), 0) == owner[...]).astype(F32).astype(BF16)
        note[...] = mm_nt(named, mine).reshape(n, 1, lanes)

    chunk = 2 * n * slots // n_det

    def fill(c):
        pick[c * chunk:(c + 1) * chunk, :] = (
            iota((chunk, 2 * tile_count), 0) + c * chunk == goal[0:1]).astype(F32).astype(BF16)

    for copy in small[2:4]:
        copy.wait()
    small[4].start()
    cov_copy.start(priority=1)
    ts_copy(0).wait()
    assign()
    project(0, half)
    scope.__exit__(None, None, None)

    row = iota((8, lanes), 0)
    left = iota((8, lanes), 1) < pix

    pending = []

    def settle(depth):
        while len(pending) > depth:
            t, out = pending.pop(0)
            even = jnp.where(row < 4, out[0:8, 0:lanes], out[0:8, lanes:])
            odds = jnp.where(row < 4, out[8:16, 0:lanes], out[8:16, lanes:])
            first = jnp.where(left, even, pltpu.roll(odds, pix, 1))
            second = jnp.where(left, pltpu.roll(even, pix, 1), odds)
            tiles[2 * t:2 * t + 8, :] = jnp.where((row // 2) % 2 == 0, first, second)

    def tile_maps(g):
        for t in range(bounds[g], bounds[g + 1], 4):
            pending.append((t, mm_nt(proj[4 * t:4 * t + 16, :], pt[t:t + 4].reshape(4 * pix, length))))
            settle(2)

    def to_plane(src, dst, sends, arrivals, z):
        for t in ((*range(0, n_tm, 2), *range(1, n_tm, 2)) if z else (*range(2, n_tm, 2), 1, 0, *range(3, n_tm, 2))):
            d = z * n_tm + t

            @pl.when(me != d)
            def _():
                pltpu.make_async_remote_copy(
                    src_ref=src.at[d], dst_ref=dst.at[me], send_sem=sends, recv_sem=arrivals,
                    device_id=(z, t), device_id_type=MESH,
                ).start()

    for g in range(stages):
        with jax.named_scope("stage%d" % g):
            if g == 1:
                ts_copy(half).wait()
                project(half, tile_count)
            if g == stages - 2:
                pl.semaphore_wait(barrier, n - 1)
                for z in range(n_det):
                    to_plane(note, notes, note_send, note_recv, z)
            pt_copy(g).wait()
            if g == stages - 2:
                for c in range(n_det):
                    fill(c)
            tile_maps(g)
    settle(0)

    payload = tiles[...].astype(BF16)
    block_rows, taps, cb = cov.shape[0], cov.shape[1], cov.shape[2]
    edges = (*range(H), *range(block_rows - H, block_rows))
    identity = (iota((cb, cb), 0) == iota((cb, cb), 1)).astype(F32).astype(BF16)

    def turn(b):
        for j in range(taps):
            turned[b * taps + j] = mm_nt(identity, cov[b, j]).astype(BF16)

    part = n_tm * slots
    side = iota((n_tm, slots // 2, lanes), 2) < pix
    for z in range(n_det):
        choice = jnp.concatenate(
            [pick[z * part:(z + 1) * part, :], pick[n * slots + z * part:n * slots + (z + 1) * part, :]], axis=0)
        out = mm(choice, payload)
        here = slice(z * n_tm, (z + 1) * n_tm)
        send[here, 0:slots, :] = out[:part].reshape(n_tm, slots, lanes).astype(BF16)
        last_rows = out[part:].reshape(n_tm, slots, lanes)
        send[here, slots:, :] = jnp.where(side, last_rows[:, :slots // 2], last_rows[:, slots // 2:]).astype(BF16)
        to_plane(send, recv, send_sem, recv_sem, z)
        if z == 0:
            small[4].wait()
            cov_copy.wait()
        for i in range(2 * H * z // n_det, 2 * H * (z + 1) // n_det):
            turn(edges[i])
    for b in range(H, block_rows - H):
        turn(b)

    notes[me] = note[me]
    recv[me] = send[me]
    ext[...] = jnp.zeros_like(ext)
    give[...] = jnp.zeros_like(give)
    others = pl.ds(0, n - 1)
    pltpu.make_async_copy(notes.at[others], notes.at[others], note_recv).wait()
    own_blocks = both.shape[2] // pix
    hb = own_blocks // 2
    entries = n * slots
    entry = iota((lanes, 3 * entries), 1)
    kind = entry // entries
    turn = entry % slots
    from_turn = jnp.where(kind == 0, turn, 2 * turn + kind - 1)
    spread = ((iota((lanes, 3 * entries), 0) == from_turn) & ((kind == 0) | (turn < slots // 2)))
    told = mm(notes[...].reshape(n, lanes).astype(BF16), spread.astype(F32).astype(BF16))
    r = iota((n, 3 * entries), 1)
    told = jnp.sum(jnp.where(iota((n, 3 * entries), 0) == (r % entries) // slots, told, 0.0), axis=0, keepdims=True)
    told = told.astype(I32)
    r = iota((own_blocks, entries), 0)
    wanted = 2 * (r % hb) + r // hb
    for k in range(3):
        hits[k * own_blocks:(k + 1) * own_blocks, :] = (
            wanted == told[:, k * entries:(k + 1) * entries]).astype(F32).astype(BF16)
    pltpu.make_async_copy(recv.at[others], recv.at[others], recv_sem).wait()

    got = recv[...].astype(F32)
    pairs = got[:, 0:slots].reshape(entries, lanes).astype(BF16)
    rest = jnp.concatenate([got[:, slots:], jnp.zeros((n, slots // 2, lanes), F32)], axis=1)
    rest = rest.reshape(entries, lanes).astype(BF16)
    total = mm(hits[0:own_blocks, :], pairs)
    third = mm(hits[own_blocks:, :], rest)
    side = iota((hb, lanes), 1) < pix
    a0, a1 = total[0:hb], total[hb:]
    l0, l1, r0, r1 = (third[hb * i:hb * (i + 1)] for i in range(4))
    planes = (
        jnp.where(side, a0, pltpu.roll(a1, pix, 1)),
        jnp.where(side, pltpu.roll(a0, pix, 1), a1),
        jnp.where(side, l0, r1) + pltpu.roll(jnp.where(side, l1, r0), pix, 1),
    )
    per = cb // lanes

    rounded = [plane.astype(BF16).astype(F32) for plane in planes]
    for s in range(3):
        for i in range(H * per):
            at = (slice(4 * (i // per) + s, 4 * (i // per) + s + 1), slice((i % per) * lanes, (i % per + 1) * lanes))
            give[0, at[0], at[1]] = rounded[s][i:i + 1]
            give[1, at[0], at[1]] = rounded[s][hb - H * per + i:hb - H * per + i + 1]

    last = n - 1

    def to_next():
        return pltpu.make_async_remote_copy(
            src_ref=give.at[1], dst_ref=halo.at[0], send_sem=halo_send[0], recv_sem=halo_recv.at[0],
            device_id=coords(lax.rem(me + 1, n)), device_id_type=MESH)

    def to_before():
        return pltpu.make_async_remote_copy(
            src_ref=give.at[0], dst_ref=halo.at[1], send_sem=halo_send[1], recv_sem=halo_recv.at[1],
            device_id=coords(lax.rem(me + n - 1, n)), device_id_type=MESH)

    @pl.when(me < last)
    def _():
        to_next().start()

    @pl.when(me > 0)
    def _():
        to_before().start()


    @pl.when(me == 0)
    def _():
        halo[0] = jnp.zeros(halo.shape[1:], F32)

    @pl.when(me == last)
    def _():
        halo[1] = jnp.zeros(halo.shape[1:], F32)

    for s in range(3):
        for i in range(hb):
            ext[H + i // per, s:s + 1, (i % per) * lanes:(i % per + 1) * lanes] = rounded[s][i:i + 1]
    for s in range(3):
        for i in range(hb):
            both[0, s:s + 1, i * lanes:(i + 1) * lanes] = planes[s][i:i + 1]
    def apply(b, at):
        acc = jnp.zeros((8, cb), F32)
        for j in range(taps):
            acc = acc + mm(ext[b + H + band[j, b]].astype(BF16), turned[b * taps + j])
        both[1, :, at] = acc[0:3]

    for b in range(H, block_rows - H):
        apply(b, slice(b * cb, (b + 1) * cb))

    def finish(k):
        @pl.when(jnp.where(k == 0, me, last - me) > 0)
        def _():
            pltpu.make_async_copy(halo.at[k], halo.at[k], halo_recv.at[k]).wait()

        for h in range(H):
            ext[k * (block_rows + H) + h, 0:3, :] = halo[k, 4 * h:4 * h + 3, :]
        for h in range(H):
            b = k * (block_rows - H) + h
            apply(b, pl.ds(pl.multiple_of(b * cb, cb), cb))

    near = 1 - me % 2
    with jax.named_scope("near"):
        finish(near)
    with jax.named_scope("far"):
        finish(1 - near)

    @pl.when(me < last)
    def _():
        to_next().wait_send()

    @pl.when(me > 0)
    def _():
        to_before().wait_send()

    sent = pl.ds(0, n - 1)
    pltpu.make_async_copy(note.at[sent], note.at[sent], note_send).wait()
    pltpu.make_async_copy(send.at[sent], send.at[sent], send_sem).wait()


def per_device(n_det, n_tm, timestream, angles, det_weight, pointing, owner, sub_block, cov, band):
    n = n_det * n_tm
    tile_count, pix, length = pointing.shape
    slots = -(-2 * tile_count // (8 * n)) * 8
    lanes = 2 * pix
    block_rows, taps, cb, _ = cov.shape
    groups = tile_count // 16
    pixels = block_rows * cb
    hbm = pl.BlockSpec(memory_space=pltpu.HBM)
    both = pl.pallas_call(
        functools.partial(kernel, n_det, n_tm, slots),
        out_shape=pltpu.VMEM((2, 3, pixels), F32),
        in_specs=[hbm] * 8,
        out_specs=pl.BlockSpec(memory_space=pltpu.VMEM),
        scratch_shapes=[
            pltpu.VMEM((1, angles.shape[0]), F32),
            pltpu.VMEM((1, angles.shape[0]), F32),
            pltpu.VMEM((1, tile_count), I32),
            pltpu.VMEM((1, tile_count), I32),
            pltpu.SMEM((taps, block_rows), I32),
            pltpu.VMEM(timestream.shape, BF16),
            pltpu.VMEM(pointing.shape, BF16),
            pltpu.VMEM(cov.shape, BF16),
            pltpu.VMEM((64, 128), BF16),
            pltpu.VMEM((4 * tile_count, length), BF16),
            pltpu.VMEM((8, 2 * tile_count), I32),
            pltpu.VMEM((2 * tile_count, lanes), F32),
            pltpu.VMEM((2 * n * slots, 2 * tile_count), BF16),
            pltpu.VMEM((n, 1, lanes), F32),
            pltpu.VMEM((n, 1, lanes), F32),
            pltpu.VMEM((3 * pixels // pix, n * slots), BF16),
            pltpu.VMEM((block_rows * taps, cb, cb), BF16),
            pltpu.VMEM((n, slots + slots // 2, lanes), BF16),
            pltpu.VMEM((n, slots + slots // 2, lanes), BF16),
            pltpu.VMEM((block_rows + 2 * H, 8, cb), F32),
            pltpu.VMEM((2, 4 * H, cb), F32),
            pltpu.VMEM((2, 4 * H, cb), F32),
            pltpu.SemaphoreType.DMA((5,)),
            pltpu.SemaphoreType.DMA((2,)),
            pltpu.SemaphoreType.DMA((groups,)),
            pltpu.SemaphoreType.DMA,
            pltpu.SemaphoreType.DMA,
            pltpu.SemaphoreType.DMA((2,)),
        ],
        compiler_params=pltpu.CompilerParams(
            collective_id=0, has_side_effects=True, vmem_limit_bytes=40 * 2**20
        ),
    )(
        *(pltpu.with_memory_space_constraint(x, pltpu.HBM) for x in (
            angles.reshape(1, -1), det_weight.reshape(1, -1), owner.reshape(1, -1), sub_block, band.T,
            timestream, pointing, cov,
        ))
    )
    return both[0], both[1]


def solution(mesh):
    in_specs = (
        P("det", "tm"),
        P("det"),
        P("det"),
        P("tm", None, None),
        P("det", "tm", None),
        P("det", "tm"),
        P(("det", "tm"), None, None, None),
        P(("det", "tm"), None),
    )
    out_specs = (P(None, ("det", "tm")), P(None, ("det", "tm")))
    return jax.shard_map(
        functools.partial(per_device, mesh.shape["det"], mesh.shape["tm"]),
        mesh=mesh, in_specs=in_specs, out_specs=out_specs, check_vma=False,
    )
```

```python
import functools

import jax
import jax.numpy as jnp
from jax import lax
from jax.experimental import pallas as pl
from jax.experimental.pallas import tpu as pltpu
from jax.sharding import PartitionSpec as P

H = 2
MESH = pl.DeviceIdType.MESH
NT = (((1,), (1,)), ((), ()))
F32 = jnp.float32
BF16 = jnp.bfloat16
I32 = jnp.int32


def iota(shape, dim):
    return lax.broadcasted_iota(I32, shape, dim)


def mm(a, b):
    return jnp.dot(a, b, preferred_element_type=F32)


def mm_nt(a, b):
    return lax.dot_general(a, b, NT, preferred_element_type=F32)


def kernel(
    n_det, n_tm, slots,
    angles_hbm, weight_hbm, owner_hbm, sub_hbm, band_hbm, ts_hbm, pt_hbm, cov_hbm,
    both,
    angles, weight, owner, sub, band,
    ts, pt, cov, diag, proj, goal, tiles, pick, note, notes, hits, turned, send, recv, ext, give, halo,
    small_sem, ts_sem, pt_sem, note_recv, recv_sem, halo_recv,
):
    n = n_det * n_tm
    tile_count = pt.shape[0]
    bounds = tuple(range(0, tile_count + 1, 16))
    stages = len(bounds) - 1
    pix = pt.shape[1]
    length = pt.shape[2]
    lanes = 2 * pix
    me = lax.axis_index("det") * n_tm + lax.axis_index("tm")

    def coords(d):
        return (d // n_tm, d % n_tm)

    cov_sem, note_send, send_sem = small_sem.at[0], small_sem.at[1], small_sem.at[2]
    halo_send = (small_sem.at[3], pt_sem.at[0])
    small = [
        pltpu.make_async_copy(a, b, small_sem.at[i])
        for i, (a, b) in enumerate((
            (angles_hbm, angles), (weight_hbm, weight), (owner_hbm, owner), (sub_hbm, sub), (band_hbm, band),
        ))
    ]
    for copy in small[:4]:
        copy.start()

    half = tile_count // 2

    def ts_copy(t):
        span = pl.ds(t * length, half * length)
        return pltpu.make_async_copy(ts_hbm.at[:, span], ts.at[:, span], ts_sem.at[t // half])

    def pt_copy(g):
        part = pl.ds(bounds[g], bounds[g + 1] - bounds[g])
        return pltpu.make_async_copy(pt_hbm.at[part], pt.at[part], pt_sem.at[g])

    cov_copy = pltpu.make_async_copy(cov_hbm, cov, cov_sem)
    ts_copy(0).start()
    pt_copy(0).start(priority=1)
    for g in range(1, stages):
        pt_copy(g).start(priority=1)
    barrier = pltpu.get_barrier_semaphore()
    with jax.named_scope("greet"):
        for d in range(n):
            @pl.when(me != d)
            def _():
                pl.semaphore_signal(barrier, inc=1, device_id=(d // n_tm, d % n_tm), device_id_type=MESH)
    with jax.named_scope("small_wait"):
        for copy in small[:2]:
            copy.wait()

    ts_copy(half).start()
    scope = jax.named_scope("prologue")
    scope.__enter__()
    row8 = iota((8, 8), 0)
    ang = jnp.broadcast_to(2.0 * angles[...], (8, 8))
    wgt = jnp.broadcast_to(weight[...], (8, 8))
    trig = jnp.where(row8 == 0, 1.0, jnp.where(row8 == 1, jnp.cos(ang), jnp.sin(ang)))
    polar = jnp.where(row8 < 3, wgt * trig, 0.0).astype(BF16)
    r = iota((64, 8), 0)
    stokes = jnp.where(r % 2 == 1, 2, (r // 8) % 2)
    spread = mm((stokes == iota((64, 8), 1)).astype(F32).astype(BF16), polar).astype(BF16)
    spread = mm(spread, (iota((8, 128), 1) % 8 == iota((8, 128), 0)).astype(F32).astype(BF16))
    r = iota((64, 128), 0)
    tile_of = 4 * (r // 16) + (r // 2) % 4
    diag[...] = jnp.where(iota((64, 128), 1) // 8 == tile_of, spread, 0.0).astype(BF16)

    def project(low_t, high_t):
        for t in range(low_t, high_t, 16):
            stream = jnp.concatenate(
                [ts[:, k * length:(k + 1) * length].astype(F32) for k in range(t, t + 16)], axis=0
            ).astype(BF16)
            proj[4 * t:4 * t + 64, :] = mm(diag[...], stream).astype(BF16)

    def assign():
        square = (tile_count, tile_count)
        dest = jnp.broadcast_to(owner[...].astype(F32), square)
        dest_column = mm_nt((iota(square, 0) == iota(square, 1)).astype(BF16), dest.astype(BF16))
        earlier = iota(square, 0) < iota(square, 1)
        rank = jnp.sum(jnp.where(earlier & (dest_column == dest), 1.0, 0.0), axis=0, keepdims=True)
        twice = (iota((tile_count, 2 * tile_count), 1) // 2 == iota((tile_count, 2 * tile_count), 0)).astype(BF16)
        pair = jnp.where(iota((8, tile_count), 0) == 0, dest[0:8], jnp.broadcast_to(rank, (8, tile_count)))
        pair = mm(pair.astype(BF16), twice).astype(I32)
        place = pair[0:1] * slots
        turn = pair[1:2]
        both_halves = n * slots + place + turn // 2 + (turn % 2) * (slots // 2)
        odd = iota((1, 2 * tile_count), 1) % 2 == 1
        goal[...] = jnp.broadcast_to(jnp.where(odd, both_halves, place + turn), (8, 2 * tile_count))
        mine = jnp.where(iota((lanes, tile_count), 0) == rank.astype(I32),
                         jnp.broadcast_to(sub[...].astype(F32), (lanes, tile_count)), 0.0).astype(BF16)
        named = (iota((n, tile_count), 0) == owner[...]).astype(F32).astype(BF16)
        note[...] = mm_nt(named, mine).reshape(n, 1, lanes)

    chunk = 2 * n * slots // n_det

    def fill(c):
        pick[c * chunk:(c + 1) * chunk, :] = (
            iota((chunk, 2 * tile_count), 0) + c * chunk == goal[0:1]).astype(F32).astype(BF16)

    for copy in small[2:4]:
        copy.wait()
    small[4].start()
    cov_copy.start(priority=1)
    ts_copy(0).wait()
    assign()
    project(0, half)
    scope.__exit__(None, None, None)

    row = iota((8, lanes), 0)
    left = iota((8, lanes), 1) < pix

    pending = []

    def settle(depth):
        while len(pending) > depth:
            t, out = pending.pop(0)
            even = jnp.where(row < 4, out[0:8, 0:lanes], out[0:8, lanes:])
            odds = jnp.where(row < 4, out[8:16, 0:lanes], out[8:16, lanes:])
            first = jnp.where(left, even, pltpu.roll(odds, pix, 1))
            second = jnp.where(left, pltpu.roll(even, pix, 1), odds)
            tiles[2 * t:2 * t + 8, :] = jnp.where((row // 2) % 2 == 0, first, second)

    def tile_maps(g):
        for t in range(bounds[g], bounds[g + 1], 4):
            pending.append((t, mm_nt(proj[4 * t:4 * t + 16, :], pt[t:t + 4].reshape(4 * pix, length))))
            settle(2)

    def to_plane(src, dst, sends, arrivals, z):
        for t in ((*range(0, n_tm, 2), *range(1, n_tm, 2)) if z else (*range(2, n_tm, 2), 1, 0, *range(3, n_tm, 2))):
            d = z * n_tm + t

            @pl.when(me != d)
            def _():
                pltpu.make_async_remote_copy(
                    src_ref=src.at[d], dst_ref=dst.at[me], send_sem=sends, recv_sem=arrivals,
                    device_id=(z, t), device_id_type=MESH,
                ).start()

    for g in range(stages):
        with jax.named_scope("stage%d" % g):
            if g == 1:
                ts_copy(half).wait()
                project(half, tile_count)
            if g == stages - 4:
                pl.semaphore_wait(barrier, n - 1)
                for z in range(n_det):
                    to_plane(note, notes, note_send, note_recv, z)
            pt_copy(g).wait()
            if g == stages - 2:
                for c in range(n_det):
                    fill(c)
            tile_maps(g)
    settle(0)

    payload = tiles[...].astype(BF16)
    block_rows, taps, cb = cov.shape[0], cov.shape[1], cov.shape[2]
    edges = (*range(H), *range(block_rows - H, block_rows))
    identity = (iota((cb, cb), 0) == iota((cb, cb), 1)).astype(F32).astype(BF16)

    def turn(b):
        for j in range(taps):
            turned[b * taps + j] = mm_nt(identity, cov[b, j]).astype(BF16)

    part = n_tm * slots
    side = iota((n_tm, slots // 2, lanes), 2) < pix
    for z in range(n_det):
        choice = jnp.concatenate(
            [pick[z * part:(z + 1) * part, :], pick[n * slots + z * part:n * slots + (z + 1) * part, :]], axis=0)
        out = mm(choice, payload)
        here = slice(z * n_tm, (z + 1) * n_tm)
        send[here, 0:slots, :] = out[:part].reshape(n_tm, slots, lanes).astype(BF16)
        last_rows = out[part:].reshape(n_tm, slots, lanes)
        send[here, slots:, :] = jnp.where(side, last_rows[:, :slots // 2], last_rows[:, slots // 2:]).astype(BF16)
        to_plane(send, recv, send_sem, recv_sem, z)
        if z == 0:
            small[4].wait()
            cov_copy.wait()
        for i in range(2 * H * z // n_det, 2 * H * (z + 1) // n_det):
            turn(edges[i])
    for b in range(H, block_rows - H):
        turn(b)

    notes[me] = note[me]
    recv[me] = send[me]
    ext[...] = jnp.zeros_like(ext)
    give[...] = jnp.zeros_like(give)
    others = pl.ds(0, n - 1)
    pltpu.make_async_copy(notes.at[others], notes.at[others], note_recv).wait()
    own_blocks = both.shape[2] // pix
    hb = own_blocks // 2
    entries = n * slots
    entry = iota((lanes, 3 * entries), 1)
    kind = entry // entries
    turn = entry % slots
    from_turn = jnp.where(kind == 0, turn, 2 * turn + kind - 1)
    spread = ((iota((lanes, 3 * entries), 0) == from_turn) & ((kind == 0) | (turn < slots // 2)))
    told = mm(notes[...].reshape(n, lanes).astype(BF16), spread.astype(F32).astype(BF16))
    r = iota((n, 3 * entries), 1)
    told = jnp.sum(jnp.where(iota((n, 3 * entries), 0) == (r % entries) // slots, told, 0.0), axis=0, keepdims=True)
    told = told.astype(I32)
    r = iota((own_blocks, entries), 0)
    wanted = 2 * (r % hb) + r // hb
    for k in range(3):
        hits[k * own_blocks:(k + 1) * own_blocks, :] = (
            wanted == told[:, k * entries:(k + 1) * entries]).astype(F32).astype(BF16)
    pltpu.make_async_copy(recv.at[others], recv.at[others], recv_sem).wait()

    got = recv[...].astype(F32)
    pairs = got[:, 0:slots].reshape(entries, lanes).astype(BF16)
    rest = jnp.concatenate([got[:, slots:], jnp.zeros((n, slots // 2, lanes), F32)], axis=1)
    rest = rest.reshape(entries, lanes).astype(BF16)
    total = mm(hits[0:own_blocks, :], pairs)
    third = mm(hits[own_blocks:, :], rest)
    side = iota((hb, lanes), 1) < pix
    a0, a1 = total[0:hb], total[hb:]
    l0, l1, r0, r1 = (third[hb * i:hb * (i + 1)] for i in range(4))
    planes = (
        jnp.where(side, a0, pltpu.roll(a1, pix, 1)),
        jnp.where(side, pltpu.roll(a0, pix, 1), a1),
        jnp.where(side, l0, r1) + pltpu.roll(jnp.where(side, l1, r0), pix, 1),
    )
    per = cb // lanes

    rounded = [plane.astype(BF16).astype(F32) for plane in planes]
    for s in range(3):
        for i in range(H * per):
            at = (slice(4 * (i // per) + s, 4 * (i // per) + s + 1), slice((i % per) * lanes, (i % per + 1) * lanes))
            give[0, at[0], at[1]] = rounded[s][i:i + 1]
            give[1, at[0], at[1]] = rounded[s][hb - H * per + i:hb - H * per + i + 1]

    last = n - 1

    def to_next():
        return pltpu.make_async_remote_copy(
            src_ref=give.at[1], dst_ref=halo.at[0], send_sem=halo_send[0], recv_sem=halo_recv.at[0],
            device_id=coords(lax.rem(me + 1, n)), device_id_type=MESH)

    def to_before():
        return pltpu.make_async_remote_copy(
            src_ref=give.at[0], dst_ref=halo.at[1], send_sem=halo_send[1], recv_sem=halo_recv.at[1],
            device_id=coords(lax.rem(me + n - 1, n)), device_id_type=MESH)

    @pl.when(me < last)
    def _():
        to_next().start()

    @pl.when(me > 0)
    def _():
        to_before().start()


    @pl.when(me == 0)
    def _():
        halo[0] = jnp.zeros(halo.shape[1:], F32)

    @pl.when(me == last)
    def _():
        halo[1] = jnp.zeros(halo.shape[1:], F32)

    for s in range(3):
        for i in range(hb):
            ext[H + i // per, s:s + 1, (i % per) * lanes:(i % per + 1) * lanes] = rounded[s][i:i + 1]
    for s in range(3):
        for i in range(hb):
            both[0, s:s + 1, i * lanes:(i + 1) * lanes] = planes[s][i:i + 1]
    def apply(b, at):
        acc = jnp.zeros((8, cb), F32)
        for j in range(taps):
            acc = acc + mm(ext[b + H + band[j, b]].astype(BF16), turned[b * taps + j])
        both[1, :, at] = acc[0:3]

    for b in range(H, block_rows - H):
        apply(b, slice(b * cb, (b + 1) * cb))

    def finish(k):
        @pl.when(jnp.where(k == 0, me, last - me) > 0)
        def _():
            pltpu.make_async_copy(halo.at[k], halo.at[k], halo_recv.at[k]).wait()

        for h in range(H):
            ext[k * (block_rows + H) + h, 0:3, :] = halo[k, 4 * h:4 * h + 3, :]
        for h in range(H):
            b = k * (block_rows - H) + h
            apply(b, pl.ds(pl.multiple_of(b * cb, cb), cb))

    near = 1 - me % 2
    with jax.named_scope("near"):
        finish(near)
    with jax.named_scope("far"):
        finish(1 - near)

    @pl.when(me < last)
    def _():
        to_next().wait_send()

    @pl.when(me > 0)
    def _():
        to_before().wait_send()

    sent = pl.ds(0, n - 1)
    pltpu.make_async_copy(note.at[sent], note.at[sent], note_send).wait()
    pltpu.make_async_copy(send.at[sent], send.at[sent], send_sem).wait()


def per_device(n_det, n_tm, timestream, angles, det_weight, pointing, owner, sub_block, cov, band):
    n = n_det * n_tm
    tile_count, pix, length = pointing.shape
    slots = -(-2 * tile_count // (8 * n)) * 8
    lanes = 2 * pix
    block_rows, taps, cb, _ = cov.shape
    groups = tile_count // 16
    pixels = block_rows * cb
    hbm = pl.BlockSpec(memory_space=pltpu.HBM)
    both = pl.pallas_call(
        functools.partial(kernel, n_det, n_tm, slots),
        out_shape=pltpu.VMEM((2, 3, pixels), F32),
        in_specs=[hbm] * 8,
        out_specs=pl.BlockSpec(memory_space=pltpu.VMEM),
        scratch_shapes=[
            pltpu.VMEM((1, angles.shape[0]), F32),
            pltpu.VMEM((1, angles.shape[0]), F32),
            pltpu.VMEM((1, tile_count), I32),
            pltpu.VMEM((1, tile_count), I32),
            pltpu.SMEM((taps, block_rows), I32),
            pltpu.VMEM(timestream.shape, BF16),
            pltpu.VMEM(pointing.shape, BF16),
            pltpu.VMEM(cov.shape, BF16),
            pltpu.VMEM((64, 128), BF16),
            pltpu.VMEM((4 * tile_count, length), BF16),
            pltpu.VMEM((8, 2 * tile_count), I32),
            pltpu.VMEM((2 * tile_count, lanes), F32),
            pltpu.VMEM((2 * n * slots, 2 * tile_count), BF16),
            pltpu.VMEM((n, 1, lanes), F32),
            pltpu.VMEM((n, 1, lanes), F32),
            pltpu.VMEM((3 * pixels // pix, n * slots), BF16),
            pltpu.VMEM((block_rows * taps, cb, cb), BF16),
            pltpu.VMEM((n, slots + slots // 2, lanes), BF16),
            pltpu.VMEM((n, slots + slots // 2, lanes), BF16),
            pltpu.VMEM((block_rows + 2 * H, 8, cb), F32),
            pltpu.VMEM((2, 4 * H, cb), F32),
            pltpu.VMEM((2, 4 * H, cb), F32),
            pltpu.SemaphoreType.DMA((5,)),
            pltpu.SemaphoreType.DMA((2,)),
            pltpu.SemaphoreType.DMA((groups,)),
            pltpu.SemaphoreType.DMA,
            pltpu.SemaphoreType.DMA,
            pltpu.SemaphoreType.DMA((2,)),
        ],
        compiler_params=pltpu.CompilerParams(
            collective_id=0, has_side_effects=True, vmem_limit_bytes=40 * 2**20
        ),
    )(
        *(pltpu.with_memory_space_constraint(x, pltpu.HBM) for x in (
            angles.reshape(1, -1), det_weight.reshape(1, -1), owner.reshape(1, -1), sub_block, band.T,
            timestream, pointing, cov,
        ))
    )
    return both[0], both[1]


def solution(mesh):
    in_specs = (
        P("det", "tm"),
        P("det"),
        P("det"),
        P("tm", None, None),
        P("det", "tm", None),
        P("det", "tm"),
        P(("det", "tm"), None, None, None),
        P(("det", "tm"), None),
    )
    out_specs = (P(None, ("det", "tm")), P(None, ("det", "tm")))
    return jax.shard_map(
        functools.partial(per_device, mesh.shape["det"], mesh.shape["tm"]),
        mesh=mesh, in_specs=in_specs, out_specs=out_specs, check_vma=False,
    )
```
